128 devices in a mesh: cand: 8 (over y, core), ctx: 16 (over x, z).
Axes of the slice: x: 4, y: 4, z: 4, core: 2. Of those that a mesh axis runs over, the one named last changes fastest.
Arguments:
- query_matrix: bfloat16 [8, 2048, 1536], P('cand', 'ctx'), as said below
- key_matrix: bfloat16 [8, 2048, 512], P('cand', 'ctx'), as said below
- value_matrix: bfloat16 [8, 2048, 512], P('cand', 'ctx'), may hold values from -6 to 6
- output_gradient: bfloat16 [8, 2048, 1536], P('cand', 'ctx'), may hold values from -6 to 6
- parent: int32 [8], replicated, may hold values from 0 to 7, as said below
- seg_depth: int32 [8], replicated, may hold values from 0 to 2, as said below
- block_mask: int32 [8, 16, 16], P('cand'), may hold values 0 or 1
Outputs:
- attended: bfloat16 [8, 2048, 1536], P('cand', 'ctx')
- query_grad: bfloat16 [8, 2048, 1536], P('cand', 'ctx')
- key_grad: bfloat16 [8, 2048, 512], P('cand', 'ctx')
- value_grad: bfloat16 [8, 2048, 512], P('cand', 'ctx')
The draws below stay inside these ranges and needn't reach their ends.
Inputs may be any that keep to these rules, and one draw needn't show every extreme that they name: `query_matrix`: query entries lie within -9 to 9. `key_matrix`: key entries lie within -6 to 6. parent[s] is the segment that segment s continues; exactly one root segment is its own parent; a child of the root has the root as parent, every other segment has a child of the root as parent. seg_depth[s] counts the ancestors of segment s: 0 for the root only, 1 for the root's children, 2 for all others.
All inputs are finite; a program needn't handle non-finite values. No bound on the sum of `block_mask` on one device may be relied on, other than what follows from the above.
Results may differ from the reference program's by a relative error of at most 0.018.
Values may be sent and summed in bfloat16 or wider, within the bound.
No kernel may reach another device: no remote copies, remote signals or barrier semaphores. Data moves between devices by JAX's collectives and lax.ppermute only.
A program may use at most 192 MiB of HBM per device.

```python
import jax
import jax.numpy as jnp
from jax import lax

QUERY_HEAD_COUNT = 12
KEY_VALUE_HEADS = 4
HEAD_SIZE = 128
BLOCK = 128
VISIBLE_SLOTS = 3
TOKENS_PER_SHARD = 128
SEGMENT_COUNT = 8
SEGMENT_LENGTH = 2048
NB = 16


def tree_shape(key):
    tree_key = jax.random.fold_in(key, 11)
    order_key, chosen_key = jax.random.split(tree_key)
    ordering = jax.random.permutation(order_key, SEGMENT_COUNT).astype(jnp.int32)
    first_level = max(1, SEGMENT_COUNT // 4)
    role_index = jnp.arange(SEGMENT_COUNT, dtype=jnp.int32)
    chosen = jax.random.randint(chosen_key, (SEGMENT_COUNT,), 1, first_level + 1).astype(jnp.int32)
    parent_role = jnp.where(role_index <= first_level, 0, chosen).astype(jnp.int32)
    depth_role = jnp.where(role_index == 0, 0, jnp.where(role_index <= first_level, 1, 2)).astype(jnp.int32)
    parent_out = jnp.zeros((SEGMENT_COUNT,), jnp.int32).at[ordering].set(ordering[parent_role])
    depth_out = jnp.zeros((SEGMENT_COUNT,), jnp.int32).at[ordering].set(depth_role)
    return (parent_out, depth_out)


def draw_parent(key, part):
    return tree_shape(key)[0]


def draw_seg_depth(key, part):
    return tree_shape(key)[1]


def draw_key_matrix(key, part):
    private_random_key = jax.random.fold_in(key, 31)
    return jnp.clip(jax.random.normal(private_random_key, (SEGMENT_COUNT, SEGMENT_LENGTH, KEY_VALUE_HEADS * HEAD_SIZE), jnp.float32), -6.0, 6.0).astype(jnp.bfloat16)


def draw_query_matrix(key, part):
    private_random_key = jax.random.fold_in(key, 37)
    return jnp.clip(jax.random.normal(private_random_key, (SEGMENT_COUNT, SEGMENT_LENGTH, QUERY_HEAD_COUNT * HEAD_SIZE), jnp.float32), -6.0, 6.0).astype(jnp.bfloat16)


def set_ends(drawn, key, smallest, top_value):
    longest = drawn.shape.index(max(drawn.shape))
    spots = []
    for shift in (0, 1):
        where = [jax.random.randint(jax.random.fold_in(key, axis), (), 0, length) for axis, length in enumerate(drawn.shape)]
        where[longest] = (where[longest] + shift) % drawn.shape[longest]
        spots.append(tuple(where))
    return drawn.at[spots[0]].set(smallest).at[spots[1]].set(top_value)


def block_scale(rng, dims, cuts, low, top_value):
    def one(position, parts):
        steps = jax.random.uniform(jax.random.fold_in(jax.random.fold_in(rng, 6), position), (parts,), jnp.float32, low / len(cuts), top_value / len(cuts))
        return jnp.repeat(jnp.exp(steps), dims[position] // parts).reshape((-1,) + (1,) * (len(dims) - position - 1))

    factor_of = one(*cuts[0])
    for cut in cuts[1:]:
        factor_of = factor_of * one(*cut)
    return factor_of


def noise(own_key, shape, spread, limit, shards=(), held_as=jnp.bfloat16):
    values = spread * jax.random.normal(own_key, shape, jnp.float32)
    if shards:
        values = values * block_scale(own_key, shape, shards, -0.22, 0.18)
    return jnp.clip(values, -limit, limit).astype(held_as)


def setup_inputs(seed: int = 0) -> dict:
    key_list = jax.random.split(jax.random.key(seed), 8)
    query_matrix = draw_query_matrix(jax.random.fold_in(key_list[7], 71), 0)
    key_matrix = draw_key_matrix(jax.random.fold_in(key_list[7], 71), 0)
    value_matrix = noise(key_list[2], (SEGMENT_COUNT, SEGMENT_LENGTH, KEY_VALUE_HEADS * HEAD_SIZE), 1.0, 6.0, ((0, 8), (1, 16)))
    output_gradient = noise(key_list[3], (SEGMENT_COUNT, SEGMENT_LENGTH, QUERY_HEAD_COUNT * HEAD_SIZE), 1.0, 6.0, ((0, 8), (1, 16)))
    parent = draw_parent(jax.random.fold_in(key_list[7], 71), 0)
    seg_depth = draw_seg_depth(jax.random.fold_in(key_list[7], 71), 0)
    block_mask = set_ends((jax.random.randint(key_list[6], (SEGMENT_COUNT, NB, NB), 0, 4) < 3).astype(jnp.int32), jax.random.fold_in(key_list[6], 1), 0, 1)
    return {"query_matrix": query_matrix, "key_matrix": key_matrix, "value_matrix": value_matrix, "output_gradient": output_gradient, "parent": parent, "seg_depth": seg_depth, "block_mask": block_mask}


negative_big = -1.0e30


def reference(query_matrix, key_matrix, value_matrix, output_gradient, parent, seg_depth, block_mask):
    query_group_width = QUERY_HEAD_COUNT // KEY_VALUE_HEADS
    scaling = HEAD_SIZE ** -0.5
    sharded_inputs = SEGMENT_LENGTH // TOKENS_PER_SHARD
    positions = jnp.arange(SEGMENT_LENGTH, dtype=jnp.int32)
    block_ids = positions // BLOCK
    causal = positions[None, :] <= positions[:, None]
    same_block = block_ids[None, :] == block_ids[:, None]

    def segment_step(state, membership_mask):
        key_acc, value_acc = state
        first_up = parent[membership_mask]
        lineage_table = jnp.stack([membership_mask, first_up, parent[first_up]]).astype(jnp.int32)
        live_slots = jnp.arange(VISIBLE_SLOTS, dtype=jnp.int32) <= seg_depth[membership_mask]
        own_mask = block_mask[membership_mask][block_ids[:, None], block_ids[None, :]]
        own_seen = causal & (same_block | (own_mask > 0))
        far_seen = jnp.broadcast_to(live_slots[None, 1:, None], (SEGMENT_LENGTH, VISIBLE_SLOTS - 1, SEGMENT_LENGTH))
        seen_mask = jnp.concatenate([own_seen[:, None, :], far_seen], axis=1)
        query_tensor = query_matrix[membership_mask].astype(jnp.float32).reshape(SEGMENT_LENGTH, KEY_VALUE_HEADS, query_group_width, HEAD_SIZE)
        gradient_tuple = output_gradient[membership_mask].astype(jnp.float32).reshape(SEGMENT_LENGTH, KEY_VALUE_HEADS, query_group_width, HEAD_SIZE)
        gathered_keys = key_matrix[lineage_table].astype(jnp.float32).reshape(VISIBLE_SLOTS, SEGMENT_LENGTH, KEY_VALUE_HEADS, HEAD_SIZE)
        gathered_values = value_matrix[lineage_table].astype(jnp.float32).reshape(VISIBLE_SLOTS, SEGMENT_LENGTH, KEY_VALUE_HEADS, HEAD_SIZE)
        raw_scores = jnp.einsum("qhgd,lkhd->hgqlk", query_tensor, gathered_keys) * scaling
        raw_scores = jnp.where(seen_mask[None, None], raw_scores, negative_big)
        row_max = jnp.max(raw_scores, axis=(3, 4))
        log_total = row_max + jnp.log(jnp.sum(jnp.exp(raw_scores - row_max[..., None, None]), axis=(3, 4)))
        weights = jnp.where(seen_mask[None, None], jnp.exp(raw_scores - log_total[..., None, None]), 0.0)
        weights_reduced = lax.optimization_barrier(weights.astype(jnp.bfloat16)).astype(jnp.float32)
        attended = jnp.einsum("hgqlk,lkhd->qhgd", weights_reduced, gathered_values).astype(jnp.bfloat16)
        attended_f = lax.optimization_barrier(attended).astype(jnp.float32)
        row_delta = jnp.einsum("qhgd,qhgd->hgq", gradient_tuple, attended_f)
        grad_weights = jnp.einsum("qhgd,lkhd->hgqlk", gradient_tuple, gathered_values)
        grad_scores = (weights * (grad_weights - row_delta[..., None, None]) * scaling).astype(jnp.bfloat16)
        gradient_reduced = lax.optimization_barrier(grad_scores).astype(jnp.float32)
        query_grad = jnp.einsum("hgqlk,lkhd->qhgd", gradient_reduced, gathered_keys).astype(jnp.bfloat16)
        gradient_pieces = gradient_reduced.reshape(KEY_VALUE_HEADS, query_group_width, sharded_inputs, TOKENS_PER_SHARD, VISIBLE_SLOTS, SEGMENT_LENGTH)
        weight_pieces = weights_reduced.reshape(KEY_VALUE_HEADS, query_group_width, sharded_inputs, TOKENS_PER_SHARD, VISIBLE_SLOTS, SEGMENT_LENGTH)
        query_pieces = query_tensor.reshape(sharded_inputs, TOKENS_PER_SHARD, KEY_VALUE_HEADS, query_group_width, HEAD_SIZE)
        cotangent_pieces = gradient_tuple.reshape(sharded_inputs, TOKENS_PER_SHARD, KEY_VALUE_HEADS, query_group_width, HEAD_SIZE)
        key_part = jnp.einsum("hgcqlk,cqhgd->clkhd", gradient_pieces, query_pieces)
        value_part = jnp.einsum("hgcqlk,cqhgd->clkhd", weight_pieces, cotangent_pieces)
        key_gradient_sum = jnp.sum(lax.optimization_barrier(key_part.astype(jnp.bfloat16)).astype(jnp.float32), axis=0)
        value_gradient_sum = jnp.sum(lax.optimization_barrier(value_part.astype(jnp.bfloat16)).astype(jnp.float32), axis=0)
        key_gradient_sum = key_gradient_sum.reshape(VISIBLE_SLOTS, SEGMENT_LENGTH, KEY_VALUE_HEADS * HEAD_SIZE)
        value_gradient_sum = value_gradient_sum.reshape(VISIBLE_SLOTS, SEGMENT_LENGTH, KEY_VALUE_HEADS * HEAD_SIZE)
        for slot in range(VISIBLE_SLOTS):
            key_acc = key_acc.at[lineage_table[slot]].add(jnp.where(live_slots[slot], key_gradient_sum[slot], jnp.float32(0.0)))
            value_acc = value_acc.at[lineage_table[slot]].add(jnp.where(live_slots[slot], value_gradient_sum[slot], jnp.float32(0.0)))
        return (key_acc, value_acc), (attended.reshape(SEGMENT_LENGTH, QUERY_HEAD_COUNT * HEAD_SIZE), query_grad.reshape(SEGMENT_LENGTH, QUERY_HEAD_COUNT * HEAD_SIZE))

    initial_state = (jnp.zeros((SEGMENT_COUNT, SEGMENT_LENGTH, KEY_VALUE_HEADS * HEAD_SIZE), jnp.float32), jnp.zeros((SEGMENT_COUNT, SEGMENT_LENGTH, KEY_VALUE_HEADS * HEAD_SIZE), jnp.float32))
    final_state, stacked = lax.scan(segment_step, initial_state, jnp.arange(SEGMENT_COUNT, dtype=jnp.int32))
    attended_all, query_all = stacked
    return (attended_all, query_all, final_state[0].astype(jnp.bfloat16), final_state[1].astype(jnp.bfloat16))
```

```python
import functools
import math

import jax
import jax.numpy as jnp
from jax import lax
from jax.experimental import pallas as pl
from jax.experimental.pallas import tpu as pltpu
from jax.sharding import PartitionSpec as P

HEAD = 128
BLOCK = 128
GROUP = 3
ROWS = GROUP * BLOCK
KVW = 2 * HEAD
CHUNK = 4
NKEY = CHUNK * BLOCK
NEG = -1e30
SCALE = HEAD ** (-0.5)
LOG2E = math.log2(math.e)


def nt(a, b):
    return lax.dot_general(a, b, (((1,), (1,)), ((), ())), preferred_element_type=jnp.float32)


def nn(a, b):
    return lax.dot_general(a, b, (((1,), (0,)), ((), ())), preferred_element_type=jnp.float32)


def attend_kernel(
    nseg, nblk, tab, bias, q_in, do_in, kva, kvb,
    o_out, dq_out, own_out, oth_out,
    kv, acc, s_buf, p_buf, mx, ls, o_acc, stage, in_sem, out_sem, tseg, tgrp,
):
    loads = []
    for y in range(nseg):
        loads.append(pltpu.make_async_copy(kva.at[:, y], kv.at[y], in_sem.at[y]))
        loads.append(pltpu.make_async_copy(kvb.at[:, y], kv.at[nseg + y], in_sem.at[nseg + y]))
    for cp in loads:
        cp.start()
    pos = tab[0]
    diag = pos // CHUNK
    far_groups = nblk // CHUNK

    @pl.loop(0, 2 * nseg)
    def _(p):
        @pl.loop(0, nblk)
        def _(b):
            acc[p, b] = jnp.zeros((KVW, BLOCK), jnp.float32)

    for cp in loads:
        cp.wait()

    def keys(p, g):
        return kv[p, pl.ds(g * CHUNK, CHUNK), :, :HEAD].reshape(NKEY, HEAD)

    def values(p, g):
        return kv[p, pl.ds(g * CHUNK, CHUNK), :, HEAD:].reshape(NKEY, HEAD)

    def lanes(op, x):
        return functools.reduce(op, [x[:, i * HEAD : (i + 1) * HEAD] for i in range(CHUNK)])

    @pl.loop(0, nseg)
    def _(j):
        qm = q_in[j]
        dm = do_in[j]
        rows_of = lambda x: jnp.concatenate([x[:, g * HEAD : (g + 1) * HEAD] for g in range(GROUP)], axis=0)
        query = rows_of(qm)
        cotan = rows_of(dm)
        query_t = jnp.concatenate([qm[:, g * HEAD : (g + 1) * HEAD].T for g in range(GROUP)], axis=1)
        nfar = tab[1 + j]

        def set_own(i, _):
            tseg[i] = j
            tgrp[i] = i
            return 0

        lax.fori_loop(0, diag + 1, set_own, 0)

        def set_far(i, _):
            tseg[diag + 1 + i] = tab[5 + (i // far_groups) * nseg + j]
            tgrp[diag + 1 + i] = lax.rem(i, far_groups)
            return 0

        lax.fori_loop(0, nfar * far_groups, set_far, 0)
        total = diag + 1 + nfar * far_groups

        mx[...] = jnp.full((ROWS, HEAD), NEG, jnp.float32)
        ls[...] = jnp.zeros((ROWS, HEAD), jnp.float32)
        o_acc[...] = jnp.zeros((ROWS, HEAD), jnp.float32)

        def put(i, s):
            s_buf[i] = s
            mx[...] = jnp.maximum(mx[...], lanes(jnp.maximum, s))

        @pl.loop(0, diag)
        def _(i):
            put(i, nt(query, keys(j, i)) + bias[j, pl.ds(i, 1)])

        @pl.when(diag >= 0)
        def _():
            row = lax.broadcasted_iota(jnp.int32, (BLOCK, NKEY), 0) + pos * BLOCK
            col = lax.broadcasted_iota(jnp.int32, (BLOCK, NKEY), 1) + diag * NKEY
            low = jnp.where(col <= row, bias[j, pl.ds(diag, 1)], NEG)
            put(diag, nt(query, keys(j, diag)) + jnp.concatenate([low] * GROUP, axis=0))

        @pl.loop(diag + 1, total)
        def _(i):
            put(i, nt(query, keys(tseg[i], tgrp[i])))

        top = jnp.max(mx[...], axis=1, keepdims=True)
        mx[...] = jnp.broadcast_to(top * (SCALE * LOG2E), (ROWS, HEAD))

        @pl.loop(0, total)
        def _(i):
            m_all = jnp.concatenate([mx[...]] * CHUNK, axis=1)
            p = jnp.exp2(s_buf[i] * (SCALE * LOG2E) - m_all)
            ls[...] += lanes(jnp.add, p)
            p_low = p.astype(jnp.bfloat16)
            p_buf[i] = p_low
            o_acc[...] += nn(p_low, values(tseg[i], tgrp[i]))

        inv = 1.0 / jnp.sum(ls[...], axis=1, keepdims=True)
        out = (o_acc[...] * inv).astype(jnp.bfloat16)
        for g in range(GROUP):
            o_out[j, :, g * HEAD : (g + 1) * HEAD] = out[g * BLOCK : (g + 1) * BLOCK]
        cot_low = (cotan.astype(jnp.float32) * inv).astype(jnp.bfloat16)
        delta = jnp.sum(cot_low.astype(jnp.float32) * out.astype(jnp.float32), axis=1, keepdims=True)
        mx[...] = jnp.broadcast_to(delta, (ROWS, HEAD))
        o_acc[...] = jnp.zeros((ROWS, HEAD), jnp.float32)
        cot_t = jnp.concatenate([cot_low[g * BLOCK : (g + 1) * BLOCK].T for g in range(GROUP)], axis=1)

        @pl.loop(0, total)
        def _(i):
            seg, grp = tseg[i], tgrp[i]
            key = keys(seg, grp)
            gw = nt(cot_low, values(seg, grp))
            d_all = jnp.concatenate([mx[...]] * CHUNK, axis=1)
            p_low = p_buf[i]
            ds = (gw - d_all).astype(jnp.bfloat16) * p_low
            o_acc[...] += nn(ds, key)
            dk = nn(query_t, ds)
            dv = nn(cot_t, p_low)
            for b in range(CHUNK):
                acc[seg, grp * CHUNK + b, :HEAD] += dk[:, b * BLOCK : (b + 1) * BLOCK]
                acc[seg, grp * CHUNK + b, HEAD:] += dv[:, b * BLOCK : (b + 1) * BLOCK]

        dq = (o_acc[...] * SCALE).astype(jnp.bfloat16)
        for g in range(GROUP):
            dq_out[j, :, g * HEAD : (g + 1) * HEAD] = dq[g * BLOCK : (g + 1) * BLOCK]

    def flush(p):
        dst = own_out.at[:, p] if p < nseg else oth_out.at[:, p - nseg]
        return pltpu.make_async_copy(stage.at[p % 2], dst, out_sem.at[p % 2])

    for p in range(2 * nseg):
        if p >= 2:
            flush(p - 2).wait()

        @pl.loop(0, nblk)
        def _(b):
            stage[p % 2, b, :HEAD] = (acc[p, b, :HEAD] * SCALE).astype(jnp.bfloat16)
            stage[p % 2, b, HEAD:] = acc[p, b, HEAD:].astype(jnp.bfloat16)

        flush(p).start()
    for p in (2 * nseg - 2, 2 * nseg - 1):
        flush(p).wait()


def attend(tab, bias, q, do, kva, kvb):
    nblk, nseg = kva.shape[0], kva.shape[1]
    far = nblk // CHUNK
    groups = 3 * far
    vm = pl.BlockSpec(memory_space=pltpu.VMEM)
    hbm = pl.BlockSpec(memory_space=pl.ANY)
    bf = jnp.bfloat16
    f32 = jnp.float32
    return pl.pallas_call(
        functools.partial(attend_kernel, nseg, nblk),
        out_shape=(
            jax.ShapeDtypeStruct((nseg, BLOCK, ROWS), bf),
            jax.ShapeDtypeStruct((nseg, BLOCK, ROWS), bf),
            jax.ShapeDtypeStruct((nblk, nseg, KVW, BLOCK), bf),
            jax.ShapeDtypeStruct((nblk, nseg, KVW, BLOCK), bf),
        ),
        in_specs=[pl.BlockSpec(memory_space=pltpu.SMEM), vm, vm, vm, hbm, hbm],
        out_specs=(vm, vm, hbm, hbm),
        scratch_shapes=[
            pltpu.VMEM((2 * nseg, nblk, BLOCK, KVW), bf),
            pltpu.VMEM((2 * nseg, nblk, KVW, BLOCK), f32),
            pltpu.VMEM((groups, ROWS, NKEY), f32),
            pltpu.VMEM((groups, ROWS, NKEY), bf),
            pltpu.VMEM((ROWS, HEAD), f32),
            pltpu.VMEM((ROWS, HEAD), f32),
            pltpu.VMEM((ROWS, HEAD), f32),
            pltpu.VMEM((2, nblk, KVW, BLOCK), bf),
            pltpu.SemaphoreType.DMA((2 * nseg,)),
            pltpu.SemaphoreType.DMA((2,)),
            pltpu.SMEM((groups,), jnp.int32),
            pltpu.SMEM((groups,), jnp.int32),
        ],
        compiler_params=pltpu.CompilerParams(vmem_limit_bytes=62 * 1024 * 1024),
        cost_estimate=pl.CostEstimate(
            flops=nseg * 3 * nblk * BLOCK * ROWS * HEAD * 12,
            bytes_accessed=4 * nseg * nblk * BLOCK * KVW * 2,
            transcendentals=nseg * 3 * nblk * BLOCK * ROWS,
        ),
    )(tab, bias, q, do, kva, kvb)


def per_device(query_matrix, key_matrix, value_matrix, output_gradient, parent, seg_depth, block_mask):
    tok = query_matrix.shape[1]
    ncand = lax.axis_size("cand")
    nctx = lax.axis_size("ctx")
    nchip = ncand // 2
    heads = key_matrix.shape[2] // HEAD
    cand = lax.axis_index("cand")
    core = cand % 2
    pos = lax.axis_index("ctx")
    same_core = [[2 * y + c for y in range(nchip)] for c in range(2)]
    partner = [(i, i ^ 1) for i in range(ncand)]

    def spread(x):
        return lax.all_to_all(x, "cand", 0, 0, axis_index_groups=same_core)

    def by_head(x, width):
        return x.reshape(tok, heads, width).transpose(1, 0, 2)

    kv_own = jnp.concatenate([by_head(key_matrix[0], HEAD), by_head(value_matrix[0], HEAD)], axis=2)
    kv_mine = spread(kv_own)
    kva = lax.all_gather(kv_mine, "ctx", axis=0)
    kvb = lax.ppermute(kva, "cand", partner)

    mask_row = lax.dynamic_index_in_dim(block_mask[0], pos, 0, keepdims=False).astype(jnp.bfloat16)
    extra = jnp.zeros((heads, 16, 2 * ROWS), jnp.bfloat16).at[:, 0, :nctx].set(mask_row[None])
    both = jnp.concatenate([by_head(query_matrix[0], ROWS), by_head(output_gradient[0], ROWS)], axis=2)
    both = spread(jnp.concatenate([both, extra], axis=1))
    q = both[:, :tok, :ROWS]
    do = both[:, :tok, ROWS:]
    rows = both[:, tok, :nctx] > 0
    rows = rows | (jnp.arange(nctx)[None, :] == pos)
    bias = jnp.where(jnp.repeat(rows, BLOCK, axis=1), 0.0, NEG).astype(jnp.float32)
    bias = bias.reshape(nchip, nctx // CHUNK, NKEY)

    segs = 2 * jnp.arange(nchip, dtype=jnp.int32) + core

    def place(s):
        return jnp.where(s % 2 == core, s // 2, nchip + s // 2)

    up = parent[segs]
    tab = jnp.concatenate(
        [pos[None], seg_depth[segs], place(up), place(parent[up])]
    ).astype(jnp.int32)

    o, dq, own, oth = attend(tab, bias, q, do, kva, kvb)

    came = lax.ppermute(oth, "cand", partner)
    part = (own.astype(jnp.float32) + came.astype(jnp.float32)).astype(jnp.bfloat16)
    summed = lax.psum_scatter(part, "ctx", scatter_dimension=0)
    kv_grad = spread(summed)
    k_grad = kv_grad[:, :HEAD].transpose(2, 0, 1).reshape(1, tok, heads * HEAD)
    v_grad = kv_grad[:, HEAD:].transpose(2, 0, 1).reshape(1, tok, heads * HEAD)
    back = spread(jnp.concatenate([o, dq], axis=2))
    o_home = back[:, :, :ROWS].transpose(1, 0, 2).reshape(1, tok, heads * ROWS)
    dq_home = back[:, :, ROWS:].transpose(1, 0, 2).reshape(1, tok, heads * ROWS)
    return o_home, dq_home, k_grad, v_grad


def solution(mesh):
    split = P("cand", "ctx", None)
    return jax.shard_map(
        per_device,
        mesh=mesh,
        in_specs=(split, split, split, split, P(), P(), P("cand", None, None)),
        out_specs=(split, split, split, split),
        check_vma=False,
    )
```

```python
import functools
import math

import jax
import jax.numpy as jnp
from jax import lax
from jax.experimental import pallas as pl
from jax.experimental.pallas import tpu as pltpu
from jax.sharding import PartitionSpec as P

HEAD = 128
BLOCK = 128
GROUP = 3
ROWS = GROUP * BLOCK
KVW = 2 * HEAD
CHUNK = 4
NKEY = CHUNK * BLOCK
NEG = -1e30
SCALE = HEAD ** (-0.5)
LOG2E = math.log2(math.e)


def nt(a, b):
    return lax.dot_general(a, b, (((1,), (1,)), ((), ())), preferred_element_type=jnp.float32)


def nn(a, b):
    return lax.dot_general(a, b, (((1,), (0,)), ((), ())), preferred_element_type=jnp.float32)


def attend_kernel(
    nseg, nblk, tab, bias, q_in, do_in, *refs
):
    pieces, refs = refs[:20], refs[20:]
    o_out, dq_out = refs[:2]
    parts, refs = refs[2:22], refs[22:]
    kv, acc, s_buf, p_buf, mx, ls, o_acc, stage, in_sem, out_sem, tseg, tgrp = refs
    side = tab[1 + 3 * nseg]
    cx, cz = tab[2 + 3 * nseg], tab[3 + 3 * nseg]

    def block_of(half, outer, inner):
        far = lax.rem((cx if half == 0 else cz) + side - outer, side)
        near = lax.rem((cz if half == 0 else cx) + side - inner, side)
        return far * side + near if half == 0 else near * side + far

    def spans(refs5):
        same, low, high, mid_a, mid_b = refs5
        found = []
        for outer, ref in ((0, same), (1, low), (3, high)):
            for inner in range(4):
                found.append((outer, inner, ref, inner))
        for inner in range(2):
            found.append((2, inner, mid_a, inner))
            found.append((2, 2 + inner, mid_b, inner))
        return found

    loads = []
    for q in range(4):
        half = q % 2
        for outer, inner, ref, at in spans(pieces[5 * q : 5 * q + 5]):
            dst = kv.at[pl.ds(2 * q, 2), block_of(half, outer, inner)]
            loads.append(pltpu.make_async_copy(ref.at[at], dst, in_sem.at[len(loads)]))
    for cp in loads:
        cp.start()
    pos = tab[0]
    diag = pos // CHUNK
    far_groups = nblk // CHUNK

    @pl.loop(0, 2 * nseg)
    def _(p):
        @pl.loop(0, nblk)
        def _(b):
            acc[p, b] = jnp.zeros((KVW, BLOCK), jnp.float32)

    for cp in loads:
        cp.wait()

    def keys(p, g):
        return kv[p, pl.ds(g * CHUNK, CHUNK), :, :HEAD].reshape(NKEY, HEAD)

    def values(p, g):
        return kv[p, pl.ds(g * CHUNK, CHUNK), :, HEAD:].reshape(NKEY, HEAD)

    def lanes(op, x):
        return functools.reduce(op, [x[:, i * HEAD : (i + 1) * HEAD] for i in range(CHUNK)])

    @pl.loop(0, nseg)
    def _(j):
        qm = q_in[j]
        dm = do_in[j]
        rows_of = lambda x: jnp.concatenate([x[:, g * HEAD : (g + 1) * HEAD] for g in range(GROUP)], axis=0)
        query = rows_of(qm)
        cotan = rows_of(dm)
        query_t = jnp.concatenate([qm[:, g * HEAD : (g + 1) * HEAD].T for g in range(GROUP)], axis=1)
        nfar = tab[1 + j]

        def set_own(i, _):
            tseg[i] = j
            tgrp[i] = i
            return 0

        lax.fori_loop(0, diag + 1, set_own, 0)

        def set_far(i, _):
            tseg[diag + 1 + i] = tab[5 + (i // far_groups) * nseg + j]
            tgrp[diag + 1 + i] = lax.rem(i, far_groups)
            return 0

        lax.fori_loop(0, nfar * far_groups, set_far, 0)
        total = diag + 1 + nfar * far_groups

        mx[...] = jnp.full((ROWS, HEAD), NEG, jnp.float32)
        ls[...] = jnp.zeros((ROWS, HEAD), jnp.float32)
        o_acc[...] = jnp.zeros((ROWS, HEAD), jnp.float32)

        def put(i, s):
            s_buf[i] = s
            mx[...] = jnp.maximum(mx[...], lanes(jnp.maximum, s))

        @pl.loop(0, diag)
        def _(i):
            put(i, nt(query, keys(j, i)) + bias[j, pl.ds(i, 1)])

        @pl.when(diag >= 0)
        def _():
            row = lax.broadcasted_iota(jnp.int32, (BLOCK, NKEY), 0) + pos * BLOCK
            col = lax.broadcasted_iota(jnp.int32, (BLOCK, NKEY), 1) + diag * NKEY
            low = jnp.where(col <= row, bias[j, pl.ds(diag, 1)], NEG)
            put(diag, nt(query, keys(j, diag)) + jnp.concatenate([low] * GROUP, axis=0))

        @pl.loop(diag + 1, total)
        def _(i):
            put(i, nt(query, keys(tseg[i], tgrp[i])))

        top = jnp.max(mx[...], axis=1, keepdims=True)
        mx[...] = jnp.broadcast_to(top * (SCALE * LOG2E), (ROWS, HEAD))

        @pl.loop(0, total)
        def _(i):
            m_all = jnp.concatenate([mx[...]] * CHUNK, axis=1)
            p = jnp.exp2(s_buf[i] * (SCALE * LOG2E) - m_all)
            ls[...] += lanes(jnp.add, p)
            p_low = p.astype(jnp.bfloat16)
            p_buf[i] = p_low
            o_acc[...] += nn(p_low, values(tseg[i], tgrp[i]))

        inv = 1.0 / jnp.sum(ls[...], axis=1, keepdims=True)
        out = (o_acc[...] * inv).astype(jnp.bfloat16)
        for g in range(GROUP):
            o_out[j, :, g * HEAD : (g + 1) * HEAD] = out[g * BLOCK : (g + 1) * BLOCK]
        cot_low = (cotan.astype(jnp.float32) * inv).astype(jnp.bfloat16)
        delta = jnp.sum(cot_low.astype(jnp.float32) * out.astype(jnp.float32), axis=1, keepdims=True)
        mx[...] = jnp.broadcast_to(delta, (ROWS, HEAD))
        o_acc[...] = jnp.zeros((ROWS, HEAD), jnp.float32)
        cot_t = jnp.concatenate([cot_low[g * BLOCK : (g + 1) * BLOCK].T for g in range(GROUP)], axis=1)

        @pl.loop(0, total)
        def _(i):
            seg, grp = tseg[i], tgrp[i]
            key = keys(seg, grp)
            gw = nt(cot_low, values(seg, grp))
            d_all = jnp.concatenate([mx[...]] * CHUNK, axis=1)
            p_low = p_buf[i]
            ds = (gw - d_all).astype(jnp.bfloat16) * p_low
            o_acc[...] += nn(ds, key)
            dk = nn(query_t, ds)
            dv = nn(cot_t, p_low)
            for b in range(CHUNK):
                acc[seg, grp * CHUNK + b, :HEAD] += dk[:, b * BLOCK : (b + 1) * BLOCK]
                acc[seg, grp * CHUNK + b, HEAD:] += dv[:, b * BLOCK : (b + 1) * BLOCK]

        dq = (o_acc[...] * SCALE).astype(jnp.bfloat16)
        for g in range(GROUP):
            dq_out[j, :, g * HEAD : (g + 1) * HEAD] = dq[g * BLOCK : (g + 1) * BLOCK]

    def flush(q):
        return [
            pltpu.make_async_copy(stage.at[q % 2, outer * 4 + inner], ref.at[at], out_sem.at[(q % 2) * 16 + outer * 4 + inner])
            for outer, inner, ref, at in spans(parts[5 * q : 5 * q + 5])
        ]

    for q in range(4):
        if q >= 2:
            for cp in flush(q - 2):
                cp.wait()
        half = q % 2

        @pl.loop(0, 16)
        def _(t):
            b = block_of(half, t // 4, lax.rem(t, 4))
            for e in range(2):
                stage[q % 2, t, e, :HEAD] = (acc[2 * q + e, b, :HEAD] * SCALE).astype(jnp.bfloat16)
                stage[q % 2, t, e, HEAD:] = acc[2 * q + e, b, HEAD:].astype(jnp.bfloat16)

        for cp in flush(q):
            cp.start()
    for q in (2, 3):
        for cp in flush(q):
            cp.wait()


def attend(tab, bias, q, do, pieces):
    nseg, nblk = q.shape[0], 16
    far = nblk // CHUNK
    groups = 3 * far
    vm = pl.BlockSpec(memory_space=pltpu.VMEM)
    hbm = pl.BlockSpec(memory_space=pl.ANY)
    bf = jnp.bfloat16
    f32 = jnp.float32
    parts = [jax.ShapeDtypeStruct((n, 2, KVW, BLOCK), bf) for n in (4, 4, 4, 2, 2)] * 4
    return pl.pallas_call(
        functools.partial(attend_kernel, nseg, nblk),
        out_shape=[jax.ShapeDtypeStruct((nseg, BLOCK, ROWS), bf)] * 2 + parts,
        in_specs=[pl.BlockSpec(memory_space=pltpu.SMEM), vm, vm, vm] + [hbm] * 20,
        out_specs=[vm, vm] + [hbm] * 20,
        scratch_shapes=[
            pltpu.VMEM((2 * nseg, nblk, BLOCK, KVW), bf),
            pltpu.VMEM((2 * nseg, nblk, KVW, BLOCK), f32),
            pltpu.VMEM((groups, ROWS, NKEY), f32),
            pltpu.VMEM((groups, ROWS, NKEY), bf),
            pltpu.VMEM((ROWS, HEAD), f32),
            pltpu.VMEM((ROWS, HEAD), f32),
            pltpu.VMEM((ROWS, HEAD), f32),
            pltpu.VMEM((2, nblk, 2, KVW, BLOCK), bf),
            pltpu.SemaphoreType.DMA((64,)),
            pltpu.SemaphoreType.DMA((32,)),
            pltpu.SMEM((groups,), jnp.int32),
            pltpu.SMEM((groups,), jnp.int32),
        ],
        compiler_params=pltpu.CompilerParams(vmem_limit_bytes=62 * 1024 * 1024),
        cost_estimate=pl.CostEstimate(
            flops=nseg * 3 * nblk * BLOCK * ROWS * HEAD * 12,
            bytes_accessed=4 * nseg * nblk * BLOCK * KVW * 2,
            transcendentals=nseg * 3 * nblk * BLOCK * ROWS,
        ),
    )(tab, bias, q, do, *pieces)


def ring(side, along_x, step):
    if along_x:
        return [(x * side + z, ((x + step) % side) * side + z) for x in range(side) for z in range(side)]
    return [(x * side + z, x * side + (z + step) % side) for x in range(side) for z in range(side)]


def gather_ring(x, side, along_x):
    up, down = ring(side, along_x, 1), ring(side, along_x, -1)
    h = x.shape[0] // 2
    low = lax.ppermute(x, "ctx", up)
    high = lax.ppermute(x, "ctx", down)
    mid_a = lax.ppermute(low[:h], "ctx", up)
    mid_b = lax.ppermute(high[h:], "ctx", down)
    return low, high, mid_a, mid_b


def add(*xs):
    return functools.reduce(jnp.add, [x.astype(jnp.float32) for x in xs]).astype(jnp.bfloat16)


def scatter_ring(same, low, high, mid_a, mid_b, side, along_x):
    up, down = ring(side, along_x, 1), ring(side, along_x, -1)
    h = mid_a[0].shape[0]
    got_b = lax.ppermute(add(*mid_b), "ctx", up)
    got_a = lax.ppermute(add(*mid_a), "ctx", down)
    to_low = jnp.concatenate([add(*[x[:h] for x in low], got_a), add(*[x[h:] for x in low])], axis=0)
    to_high = jnp.concatenate([add(*[x[:h] for x in high]), add(*[x[h:] for x in high], got_b)], axis=0)
    got_low = lax.ppermute(to_low, "ctx", down)
    got_high = lax.ppermute(to_high, "ctx", up)
    return add(*same, got_low, got_high)


def per_device(query_matrix, key_matrix, value_matrix, output_gradient, parent, seg_depth, block_mask):
    tok = query_matrix.shape[1]
    ncand = lax.axis_size("cand")
    nctx = lax.axis_size("ctx")
    nchip = ncand // 2
    heads = key_matrix.shape[2] // HEAD
    cand = lax.axis_index("cand")
    core = cand % 2
    pos = lax.axis_index("ctx")
    same_core = [[2 * y + c for y in range(nchip)] for c in range(2)]
    partner = [(i, i ^ 1) for i in range(ncand)]

    def spread(x):
        return lax.all_to_all(x, "cand", 0, 0, axis_index_groups=same_core)

    def by_head(x, width):
        return x.reshape(tok, heads, width).transpose(1, 0, 2)

    kv_own = jnp.concatenate([by_head(key_matrix[0], HEAD), by_head(value_matrix[0], HEAD)], axis=2)
    kv_mine = spread(kv_own)
    side = math.isqrt(nctx)
    mine = []
    for half in range(2):
        along = half == 1
        one = kv_mine[2 * half : 2 * half + 2]
        low, high, mid_a, mid_b = gather_ring(one, side, along)
        line = jnp.stack([one, low, jnp.concatenate([mid_a, mid_b], axis=0), high])
        mine += [line, *gather_ring(line, side, not along)]
    pieces = mine + [lax.ppermute(x, "cand", partner) for x in mine]

    mask_row = lax.dynamic_index_in_dim(block_mask[0], pos, 0, keepdims=False).astype(jnp.bfloat16)
    extra = jnp.zeros((heads, 16, 2 * ROWS), jnp.bfloat16).at[:, 0, :nctx].set(mask_row[None])
    both = jnp.concatenate([by_head(query_matrix[0], ROWS), by_head(output_gradient[0], ROWS)], axis=2)
    both = spread(jnp.concatenate([both, extra], axis=1))
    q = both[:, :tok, :ROWS]
    do = both[:, :tok, ROWS:]
    rows = both[:, tok, :nctx] > 0
    rows = rows | (jnp.arange(nctx)[None, :] == pos)
    bias = jnp.where(jnp.repeat(rows, BLOCK, axis=1), 0.0, NEG).astype(jnp.float32)
    bias = bias.reshape(nchip, nctx // CHUNK, NKEY)

    segs = 2 * jnp.arange(nchip, dtype=jnp.int32) + core

    def place(s):
        return jnp.where(s % 2 == core, s // 2, nchip + s // 2)

    up = parent[segs]
    tab = jnp.concatenate(
        [pos[None], seg_depth[segs], place(up), place(parent[up]), jnp.stack([jnp.int32(side), pos // side, pos % side])]
    ).astype(jnp.int32)

    o, dq, *parts = attend(tab, bias, q, do, pieces)

    own, oth = parts[:10], parts[10:]
    came = [lax.ppermute(x, "cand", partner) for x in oth]
    sums = []
    for half in range(2):
        along = half == 1
        outer = scatter_ring(*zip(own[5 * half : 5 * half + 5], came[5 * half : 5 * half + 5]), side, not along)
        sums.append(
            scatter_ring((outer[0],), (outer[1],), (outer[3],), (outer[2, :1],), (outer[2, 1:],), side, along)
        )
    summed = jnp.concatenate(sums, axis=0)
    kv_grad = spread(summed)
    k_grad = kv_grad[:, :HEAD].transpose(2, 0, 1).reshape(1, tok, heads * HEAD)
    v_grad = kv_grad[:, HEAD:].transpose(2, 0, 1).reshape(1, tok, heads * HEAD)
    back = spread(jnp.concatenate([o, dq], axis=2))
    o_home = back[:, :, :ROWS].transpose(1, 0, 2).reshape(1, tok, heads * ROWS)
    dq_home = back[:, :, ROWS:].transpose(1, 0, 2).reshape(1, tok, heads * ROWS)
    return o_home, dq_home, k_grad, v_grad


def solution(mesh):
    split = P("cand", "ctx", None)
    return jax.shard_map(
        per_device,
        mesh=mesh,
        in_specs=(split, split, split, split, P(), P(), P("cand", None, None)),
        out_specs=(split, split, split, split),
        check_vma=False,
    )
```

```python
import functools
import math

import jax
import jax.numpy as jnp
from jax import lax
from jax.experimental import pallas as pl
from jax.experimental.pallas import tpu as pltpu
from jax.sharding import PartitionSpec as P


HEAD = 128
BLOCK = 128
GROUP = 3
ROWS = GROUP * BLOCK
KVW = 2 * HEAD
CHUNK = 8
NKEY = CHUNK * BLOCK
HALF = 4
HKEY = HALF * BLOCK
EXTRA = 16
NEG = -1e30
SCALE = HEAD ** (-0.5)
LOG2E = math.log2(math.e)
SAFE = 70.0


def nt(a, b):
    return lax.dot_general(a, b, (((1,), (1,)), ((), ())), preferred_element_type=jnp.float32)


def nn(a, b):
    return lax.dot_general(a, b, (((1,), (0,)), ((), ())), preferred_element_type=jnp.float32)


OUTER = (0, 0, 1, 1, 3, 3, 2, 2)


def spans(refs):
    return [(OUTER[k], 2 * (k % 2) + e, ref, e) for k, ref in enumerate(refs) for e in range(2)]


def attend_kernel(nseg, nblk, side, ids, parent, depth, both, *refs):
    pieces, refs = refs[:16], refs[16:]
    o_out, dq_out = refs[:2]
    parts, refs = refs[2:18], refs[18:]
    kv, acc, s_buf, p_buf, bias, mx, ls, o_acc, stage, in_sem, out_sem, tseg, tgrp = refs
    core = lax.rem(ids[0], 2)
    pos = ids[1]
    cx, cz = lax.div(pos, side), lax.rem(pos, side)

    def block_of(route, outer, inner):
        a = lax.rem(jnp.where(route == 0, cx, cz) + side - outer, side)
        b = lax.rem(jnp.where(route == 0, cz, cx) + side - inner, side)
        return jnp.where(route == 0, a * side + b, b * side + a)

    def place(s):
        return lax.div(s, 2) + jnp.where(lax.rem(s, 2) == core, 0, nseg)

    loads = []
    for w in range(2):
        route = core if w == 0 else 1 - core
        for outer, inner, ref, at in spans(pieces[8 * w : 8 * w + 8]):
            dst = kv.at[pl.ds(nseg * w, nseg), block_of(route, outer, inner)]
            loads.append(pltpu.make_async_copy(ref.at[at], dst, in_sem.at[len(loads)]))
    for cp in loads:
        cp.start()
    diag = lax.div(pos, CHUNK)
    far_groups = nblk // CHUNK

    @pl.loop(0, 2 * nseg)
    def _(p):
        @pl.loop(0, nblk // 4)
        def _(b):
            for e in range(4):
                acc[p, 4 * b + e] = jnp.zeros((KVW, BLOCK), jnp.float32)

    for cp in loads:
        cp.wait()

    def norm_step(p, top):
        k = jnp.max(jnp.abs(kv[p, :, :, :HEAD].reshape(nblk * BLOCK // 16, 16, HEAD)), axis=0).astype(jnp.float32)
        k = jnp.max(k, axis=0, keepdims=True)
        return jnp.maximum(top, jnp.sum(k * k, axis=1, keepdims=True))

    key_top = lax.fori_loop(0, 2 * nseg, norm_step, jnp.zeros((1, 1), jnp.float32))

    def keys(p, g, h):
        return kv[p, pl.ds(g * CHUNK + h * HALF, HALF), :, :HEAD].reshape(HKEY, HEAD)

    def values(p, g, h):
        return kv[p, pl.ds(g * CHUNK + h * HALF, HALF), :, HEAD:].reshape(HKEY, HEAD)

    def lanes(op, x):
        return functools.reduce(op, [x[:, i * HEAD : (i + 1) * HEAD] for i in range(HALF)])

    halves = CHUNK // HALF

    @pl.loop(0, nseg)
    def _(j):
        qm = both[j, :BLOCK, :ROWS]
        dm = both[j, :BLOCK, ROWS:]
        rows_of = lambda x: jnp.concatenate([x[:, g * HEAD : (g + 1) * HEAD] for g in range(GROUP)], axis=0)
        query = rows_of(qm)
        cotan = rows_of(dm)
        query_t = jnp.concatenate([qm[:, g * HEAD : (g + 1) * HEAD].T for g in range(GROUP)], axis=1)
        me = 2 * j + core
        nfar = depth[me]
        up = parent[me]
        far_a, far_b = place(up), place(parent[up])

        def set_own(i, _):
            tseg[i] = j
            tgrp[i] = i
            return 0

        lax.fori_loop(0, diag + 1, set_own, 0)

        def set_far(i, _):
            tseg[diag + 1 + i] = jnp.where(i < far_groups, far_a, far_b)
            tgrp[diag + 1 + i] = lax.rem(i, far_groups)
            return 0

        lax.fori_loop(0, nfar * far_groups, set_far, 0)
        total = diag + 1 + nfar * far_groups

        mask_row = both[j, BLOCK : BLOCK + EXTRA, :HEAD][:1].astype(jnp.float32)
        lane = lax.broadcasted_iota(jnp.int32, (1, HEAD), 1)
        for b in range(nblk):
            bit = jnp.sum(jnp.where(lane == b, mask_row, 0.0), axis=1, keepdims=True)
            open_ = jnp.broadcast_to(bit, (1, BLOCK)) + jnp.where(pos == b, 1.0, 0.0)
            bias[b // HALF, :, (b % HALF) * BLOCK : (b % HALF + 1) * BLOCK] = jnp.where(open_ > 0.5, 0.0, NEG)

        ls[...] = jnp.zeros((ROWS, HEAD), jnp.float32)
        o_acc[...] = jnp.zeros((ROWS, HEAD), jnp.float32)

        qf = query.astype(jnp.float32)
        q_top = jnp.max(jnp.sum(qf * qf, axis=1, keepdims=True), axis=0, keepdims=True)
        small = jnp.max(q_top * key_top * (SCALE * SCALE)) <= SAFE * SAFE

        def low_half(i, h):
            row = lax.broadcasted_iota(jnp.int32, (BLOCK, HKEY), 0) + pos * BLOCK
            col = lax.broadcasted_iota(jnp.int32, (BLOCK, HKEY), 1) + (i * NKEY + h * HKEY)
            low = jnp.where(col <= row, bias[i * halves + h], NEG)
            return jnp.concatenate([low] * GROUP, axis=0)

        def scores(i, seg, grp, h, kind):
            s = nt(query, keys(seg, grp, h))
            if kind == 1:
                s = s + bias[i * halves + h]
            if kind == 2:
                s = s + low_half(i, h)
            return s

        def finish(i, seg, grp, h, p):
            ls[...] += lanes(jnp.add, p)
            p_low = p.astype(jnp.bfloat16)
            p_buf[i, :, h * HKEY : (h + 1) * HKEY] = p_low
            o_acc[...] += nn(p_low, values(seg, grp, h))

        def sweep(body):
            @pl.loop(0, diag)
            def _(i):
                body(i, j, i, 1)

            body(diag, j, diag, 2)

            @pl.loop(diag + 1, total)
            def _(i):
                body(i, tseg[i], tgrp[i], 0)

        @pl.when(small)
        def _():
            def body(i, seg, grp, kind):
                for h in range(halves):
                    s = scores(i, seg, grp, h, kind)
                    finish(i, seg, grp, h, jnp.exp2(s * (SCALE * LOG2E)))

            sweep(body)

        @pl.when(jnp.logical_not(small))
        def _():
            mx[...] = jnp.full((ROWS, HEAD), NEG, jnp.float32)

            def body(i, seg, grp, kind):
                for h in range(halves):
                    s = scores(i, seg, grp, h, kind)
                    s_buf[i, :, h * HKEY : (h + 1) * HKEY] = s
                    mx[...] = jnp.maximum(mx[...], lanes(jnp.maximum, s))

            sweep(body)
            top = jnp.max(mx[...], axis=1, keepdims=True)
            mx[...] = jnp.broadcast_to(top, (ROWS, HEAD))

            @pl.loop(0, total)
            def _(i):
                m_all = jnp.concatenate([mx[...]] * HALF, axis=1)
                for h in range(halves):
                    s = s_buf[i, :, h * HKEY : (h + 1) * HKEY]
                    finish(i, tseg[i], tgrp[i], h, jnp.exp2((s - m_all) * (SCALE * LOG2E)))

        inv = 1.0 / jnp.sum(ls[...], axis=1, keepdims=True)
        out = (o_acc[...] * inv).astype(jnp.bfloat16)
        for g in range(GROUP):
            o_out[j, :, g * HEAD : (g + 1) * HEAD] = out[g * BLOCK : (g + 1) * BLOCK]
        cot_low = (cotan.astype(jnp.float32) * inv).astype(jnp.bfloat16)
        delta = jnp.sum(cot_low.astype(jnp.float32) * out.astype(jnp.float32), axis=1, keepdims=True)
        mx[...] = jnp.broadcast_to(delta, (ROWS, HEAD))
        o_acc[...] = jnp.zeros((ROWS, HEAD), jnp.float32)
        cot_t = jnp.concatenate([cot_low[g * BLOCK : (g + 1) * BLOCK].T for g in range(GROUP)], axis=1)

        @pl.loop(0, total)
        def _(i):
            seg, grp = tseg[i], tgrp[i]
            for h in range(halves):
                key = keys(seg, grp, h)
                gw = nt(cot_low, values(seg, grp, h))
                d_all = jnp.concatenate([mx[...]] * HALF, axis=1)
                p_low = p_buf[i, :, h * HKEY : (h + 1) * HKEY]
                ds = (gw - d_all).astype(jnp.bfloat16) * p_low
                o_acc[...] += nn(ds, key)
                dk = nn(query_t, ds)
                dv = nn(cot_t, p_low)
                for b in range(HALF):
                    at = grp * CHUNK + h * HALF + b
                    acc[seg, at, :HEAD] += dk[:, b * BLOCK : (b + 1) * BLOCK]
                    acc[seg, at, HEAD:] += dv[:, b * BLOCK : (b + 1) * BLOCK]

        dq = (o_acc[...] * SCALE).astype(jnp.bfloat16)
        for g in range(GROUP):
            dq_out[j, :, g * HEAD : (g + 1) * HEAD] = dq[g * BLOCK : (g + 1) * BLOCK]

    flushes = []
    for w in (1, 0):
        route = core if w == 0 else 1 - core
        for outer, inner, ref, at in spans(parts[8 * w : 8 * w + 8]):
            src = stage.at[w, outer * 4 + inner]
            flushes.append(pltpu.make_async_copy(src, ref.at[at], out_sem.at[len(flushes)]))

        @pl.loop(0, nblk)
        def _(t):
            b = block_of(route, lax.div(t, 4), lax.rem(t, 4))
            for e in range(nseg):
                stage[w, t, e, :HEAD] = (acc[nseg * w + e, b, :HEAD] * SCALE).astype(jnp.bfloat16)
                stage[w, t, e, HEAD:] = acc[nseg * w + e, b, HEAD:].astype(jnp.bfloat16)

        for cp in flushes[-16:]:
            cp.start()
    for cp in flushes:
        cp.wait()


def attend(ids, parent, depth, both, pieces, side):
    nseg, nblk = both.shape[0], side * side
    groups = 3 * (nblk // CHUNK)
    vm = pl.BlockSpec(memory_space=pltpu.VMEM)
    hbm = pl.BlockSpec(memory_space=pl.ANY)
    sm = pl.BlockSpec(memory_space=pltpu.SMEM)
    bf = jnp.bfloat16
    f32 = jnp.float32
    parts = [jax.ShapeDtypeStruct((2, nseg, KVW, BLOCK), bf)] * 16
    return pl.pallas_call(
        functools.partial(attend_kernel, nseg, nblk, side),
        out_shape=[jax.ShapeDtypeStruct((nseg, BLOCK, ROWS), bf)] * 2 + parts,
        in_specs=[sm, sm, sm, vm] + [hbm] * 16,
        out_specs=[vm, vm] + [hbm] * 16,
        scratch_shapes=[
            pltpu.VMEM((2 * nseg, nblk, BLOCK, KVW), bf),
            pltpu.VMEM((2 * nseg, nblk, KVW, BLOCK), f32),
            pltpu.VMEM((groups, ROWS, NKEY), f32),
            pltpu.VMEM((groups, ROWS, NKEY), bf),
            pltpu.VMEM((nblk // HALF, 1, HKEY), f32),
            pltpu.VMEM((ROWS, HEAD), f32),
            pltpu.VMEM((ROWS, HEAD), f32),
            pltpu.VMEM((ROWS, HEAD), f32),
            pltpu.VMEM((2, nblk, nseg, KVW, BLOCK), bf),
            pltpu.SemaphoreType.DMA((32,)),
            pltpu.SemaphoreType.DMA((32,)),
            pltpu.SMEM((groups,), jnp.int32),
            pltpu.SMEM((groups,), jnp.int32),
        ],
        compiler_params=pltpu.CompilerParams(vmem_limit_bytes=62 * 1024 * 1024),
        cost_estimate=pl.CostEstimate(
            flops=nseg * 3 * nblk * BLOCK * ROWS * HEAD * 12,
            bytes_accessed=4 * nseg * nblk * BLOCK * KVW * 2,
            transcendentals=nseg * 3 * nblk * BLOCK * ROWS,
        ),
    )(ids, parent, depth, both, *pieces)


BOTH_AXES = ("cand", "ctx")


def ring(ncand, side, phase, step):
    pairs = []
    for c in range(ncand):
        along_x = (c % 2 == 1) == (phase == 0)
        for x in range(side):
            for z in range(side):
                to = ((x + step) % side, z) if along_x else (x, (z + step) % side)
                pairs.append(((c * side + x) * side + z, (c * side + to[0]) * side + to[1]))
    return pairs


def add(*xs):
    return functools.reduce(jnp.add, [x.astype(jnp.float32) for x in xs]).astype(jnp.bfloat16)


def hop(x, perm):
    return lax.ppermute(x, BOTH_AXES, perm)


def gather_ring(line_lo, line_hi, up, down):
    low_a = hop(line_lo, up)
    high_b = hop(line_hi, down)
    low_b = hop(line_hi, up)
    high_a = hop(line_lo, down)
    mid_a = hop(low_a, up)
    mid_b = hop(high_b, down)
    return [line_lo, line_hi, low_a, low_b, high_a, high_b, mid_a, mid_b]


def scatter_ring(own, came, up, down):
    same_lo, same_hi, low_a, low_b, high_a, high_b, mid_a, mid_b = zip(own, came)
    far_b, far_a = add(*mid_b), add(*mid_a)
    got_b = hop(far_b, up)
    got_a = hop(far_a, down)
    free_b, free_a = add(*low_b), add(*high_a)
    from_b = hop(free_b, down)
    from_a = hop(free_a, up)
    last_a, last_b = add(*low_a, got_a), add(*high_b, got_b)
    end_a = hop(last_a, down)
    end_b = hop(last_b, up)
    return add(*same_lo, from_a, end_a), add(*same_hi, from_b, end_b)


def per_device(query_matrix, key_matrix, value_matrix, output_gradient, parent, seg_depth, block_mask):
    tok = query_matrix.shape[1]
    ncand = lax.axis_size("cand")
    nctx = lax.axis_size("ctx")
    nchip = ncand // 2
    heads = key_matrix.shape[2] // HEAD
    side = math.isqrt(nctx)
    pos = lax.axis_index("ctx")
    same_core = [[2 * y + c for y in range(nchip)] for c in range(2)]
    partner = [(i, i ^ 1) for i in range(ncand)]
    across = ring(ncand, side, 0, 2)
    rings = [(ring(ncand, side, phase, 1), ring(ncand, side, phase, -1)) for phase in range(2)]

    def spread(x):
        return lax.all_to_all(x, "cand", 0, 0, axis_index_groups=same_core)

    def cut(x, h, width):
        return x[:, h * width : (h + 1) * width]

    kv_own = jnp.stack(
        [
            jnp.concatenate([cut(key_matrix[0], h, HEAD), cut(value_matrix[0], h, HEAD)], axis=1)
            for h in range(heads)
        ]
    )
    kv_mine = spread(kv_own)
    near_low = hop(kv_mine, rings[0][0])
    near_high = hop(kv_mine, rings[0][1])
    opposite = hop(kv_mine, across)
    mine = gather_ring(jnp.stack([kv_mine, near_low]), jnp.stack([opposite, near_high]), *rings[1])
    pieces = mine + [lax.ppermute(x, "cand", partner) for x in mine]

    mask_row = lax.dynamic_index_in_dim(block_mask[0], pos, 0, keepdims=True).astype(jnp.bfloat16)
    extra = jnp.pad(mask_row, ((0, EXTRA - 1), (0, 2 * ROWS - nctx)))
    both = jnp.stack(
        [
            jnp.concatenate(
                [
                    jnp.concatenate(
                        [cut(query_matrix[0], h, ROWS), cut(output_gradient[0], h, ROWS)], axis=1
                    ),
                    extra,
                ],
                axis=0,
            )
            for h in range(heads)
        ]
    )
    both = spread(both)

    ids = jnp.stack([lax.axis_index("cand"), pos]).astype(jnp.int32)
    o, dq, *parts = attend(ids, parent, seg_depth, both, pieces, side)

    own, oth = parts[:8], parts[8:]
    came = [lax.ppermute(x, "cand", partner) for x in oth]
    line_lo, line_hi = scatter_ring(own, came, *rings[1])
    end_low = hop(line_lo[1], rings[0][1])
    end_high = hop(line_hi[1], rings[0][0])
    end_far = hop(line_hi[0], across)
    summed = add(line_lo[0], end_low, end_high, end_far)
    kv_grad = spread(summed)
    k_grad = kv_grad[:, :HEAD].transpose(2, 0, 1).reshape(1, tok, heads * HEAD)
    v_grad = kv_grad[:, HEAD:].transpose(2, 0, 1).reshape(1, tok, heads * HEAD)
    back = jnp.concatenate([o, dq], axis=2)
    back = spread(back)
    o_home = jnp.concatenate([back[h, :, :ROWS] for h in range(heads)], axis=1)[None]
    dq_home = jnp.concatenate([back[h, :, ROWS:] for h in range(heads)], axis=1)[None]
    return o_home, dq_home, k_grad, v_grad


def solution(mesh):
    split = P("cand", "ctx", None)
    return jax.shard_map(
        per_device,
        mesh=mesh,
        in_specs=(split, split, split, split, P(), P(), P("cand", None, None)),
        out_specs=(split, split, split, split),
        check_vma=False,
    )
```

```python
import functools
import math

import jax
import jax.numpy as jnp
from jax import lax
from jax.experimental import pallas as pl
from jax.experimental.pallas import tpu as pltpu
from jax.sharding import PartitionSpec as P


HEAD = 128
BLOCK = 128
GROUP = 3
ROWS = GROUP * BLOCK
KVW = 2 * HEAD
CHUNK = 4
NKEY = CHUNK * BLOCK
EXTRA = 16
NEG = -1e30
SCALE = HEAD ** (-0.5)
LOG2E = math.log2(math.e)
SAFE = 70.0


def nt(a, b):
    return lax.dot_general(a, b, (((1,), (1,)), ((), ())), preferred_element_type=jnp.float32)


def nn(a, b):
    return lax.dot_general(a, b, (((1,), (0,)), ((), ())), preferred_element_type=jnp.float32)


OUTER = (0, 0, 1, 1, 3, 3, 2, 2)


def spans(refs):
    return [(OUTER[k], 2 * (k % 2) + e, ref, e) for k, ref in enumerate(refs) for e in range(2)]


def attend_kernel(nseg, nblk, side, ids, parent, depth, both, *refs):
    pieces, refs = refs[:16], refs[16:]
    o_out, dq_out = refs[:2]
    parts, refs = refs[2:18], refs[18:]
    kv, acc, s_buf, p_buf, mx, ls, o_acc, q_rows, d_rows, q_cols, d_cols, stage, in_sem, out_sem, tseg, tblk = refs
    core = lax.rem(ids[0], 2)
    pos = ids[1]
    cx, cz = lax.div(pos, side), lax.rem(pos, side)

    def block_of(route, outer, inner):
        a = lax.rem(jnp.where(route == 0, cx, cz) + side - outer, side)
        b = lax.rem(jnp.where(route == 0, cz, cx) + side - inner, side)
        return jnp.where(route == 0, a * side + b, b * side + a)

    def place(s):
        return lax.div(s, 2) + jnp.where(lax.rem(s, 2) == core, 0, nseg)

    loads = []
    for w in range(2):
        route = core if w == 0 else 1 - core
        for outer, inner, ref, at in spans(pieces[8 * w : 8 * w + 8]):
            dst = kv.at[pl.ds(nseg * w, nseg), block_of(route, outer, inner)]
            loads.append(pltpu.make_async_copy(ref.at[at], dst, in_sem.at[len(loads)]))
    for cp in loads:
        cp.start()
    far_groups = nblk // CHUNK

    @pl.loop(0, 2 * nseg)
    def _(p):
        @pl.loop(0, nblk // 4)
        def _(b):
            for e in range(4):
                acc[p, 4 * b + e] = jnp.zeros((KVW, BLOCK), jnp.float32)

    def norm_step(p, top):
        k = jnp.max(jnp.abs(kv[p, :, :, :HEAD].reshape(nblk * BLOCK // 16, 16, HEAD)), axis=0).astype(jnp.float32)
        k = jnp.max(k, axis=0, keepdims=True)
        return jnp.maximum(top, jnp.sum(k * k, axis=1, keepdims=True))

    key_top = jnp.zeros((1, 1), jnp.float32)
    for w in range(2):
        for cp in loads[nblk * w : nblk * (w + 1)]:
            cp.wait()
        key_top = lax.fori_loop(nseg * w, nseg * (w + 1), norm_step, key_top)

    def source(i, far, lo):
        if far:
            return kv[tseg[i], pl.ds(tblk[CHUNK * i], CHUNK), :, lo : lo + HEAD].reshape(NKEY, HEAD)
        at = [jnp.minimum(tblk[CHUNK * i + e], nblk - 1) for e in range(CHUNK)]
        return jnp.concatenate([kv[tseg[i], b, :, lo : lo + HEAD] for b in at], axis=0)

    def keys(i, far):
        return source(i, far, 0)

    def values(i, far):
        return source(i, far, HEAD)

    def lanes(op, x):
        return functools.reduce(op, [x[:, i * HEAD : (i + 1) * HEAD] for i in range(CHUNK)])

    @pl.loop(0, nseg)
    def _(j):
        qm = both[j, :BLOCK, :ROWS]
        dm = both[j, :BLOCK, ROWS:]
        rows_of = lambda x: jnp.concatenate([x[:, g * HEAD : (g + 1) * HEAD] for g in range(GROUP)], axis=0)
        query = rows_of(qm)
        cotan = rows_of(dm)
        q_rows[...] = query
        q_cols[...] = jnp.concatenate([qm[:, g * HEAD : (g + 1) * HEAD].T for g in range(GROUP)], axis=1)
        me = 2 * j + core
        nfar = depth[me]
        up = parent[me]
        far_a, far_b = place(up), place(parent[up])

        mask_row = both[j, BLOCK : BLOCK + EXTRA, :HEAD][:1].astype(jnp.float32)
        lane = lax.broadcasted_iota(jnp.int32, (1, HEAD), 1)
        bit = jnp.where((lane < nblk) & (mask_row > 0.5), jnp.left_shift(1, jnp.minimum(lane, nblk)), 0)
        code = jnp.sum(bit.astype(jnp.float32)).astype(jnp.int32)

        def add_own(b, n):
            tblk[n] = b
            return n + lax.rem(jnp.right_shift(code, b), 2)

        seen = lax.fori_loop(0, pos, add_own, jnp.int32(0))
        own = lax.div(seen, CHUNK) + 1
        tail = seen - (own - 1) * CHUNK

        def add_tail(n, _):
            tblk[n] = jnp.where(n == seen, pos, nblk)
            return 0

        lax.fori_loop(seen, own * CHUNK, add_tail, 0)
        total = own + nfar * far_groups

        def add_seg(i, _):
            tseg[i] = jnp.where(i < own, j, jnp.where(i < own + far_groups, far_a, far_b))
            return 0

        lax.fori_loop(0, total, add_seg, 0)

        def add_far(n, _):
            tblk[(own + n) * CHUNK] = lax.rem(n, far_groups) * CHUNK
            return 0

        lax.fori_loop(0, nfar * far_groups, add_far, 0)

        ls[...] = jnp.zeros((ROWS, HEAD), jnp.float32)
        o_acc[...] = jnp.zeros((ROWS, HEAD), jnp.float32)

        qf = query.astype(jnp.float32)
        q_top = jnp.max(jnp.sum(qf * qf, axis=1, keepdims=True), axis=0, keepdims=True)
        small = jnp.max(q_top * key_top * (SCALE * SCALE)) <= SAFE * SAFE

        def scores(i, masked, far):
            s = nt(q_rows[...], keys(i, far))
            if masked:
                row = lax.broadcasted_iota(jnp.int32, (BLOCK, NKEY), 0)
                col = lax.broadcasted_iota(jnp.int32, (BLOCK, NKEY), 1)
                low = jnp.where(col <= row + tail * BLOCK, 0.0, NEG)
                s = s + jnp.concatenate([low] * GROUP, axis=0)
            return s

        def finish(i, far, p):
            ls[...] += lanes(jnp.add, p)
            p_low = p.astype(jnp.bfloat16)
            p_buf[i] = p_low
            o_acc[...] += nn(p_low, values(i, far))

        def both_kinds(body):
            @pl.loop(0, own)
            def _(i):
                body(i, False)

            @pl.loop(own, total)
            def _(i):
                body(i, True)

        def sweep(body):
            body(own - 1, True, False)

            @pl.loop(0, own - 1)
            def _(i):
                body(i, False, False)

            @pl.loop(own, total)
            def _(i):
                body(i, False, True)

        @pl.when(small)
        def _():
            sweep(lambda i, masked, far: finish(i, far, jnp.exp2(scores(i, masked, far) * (SCALE * LOG2E))))

        @pl.when(jnp.logical_not(small))
        def _():
            mx[...] = jnp.full((ROWS, HEAD), NEG, jnp.float32)

            def body(i, masked, far):
                s = scores(i, masked, far)
                s_buf[i] = s
                mx[...] = jnp.maximum(mx[...], lanes(jnp.maximum, s))

            sweep(body)
            top = jnp.max(mx[...], axis=1, keepdims=True)
            mx[...] = jnp.broadcast_to(top, (ROWS, HEAD))

            def weigh(i, far):
                m_all = jnp.concatenate([mx[...]] * CHUNK, axis=1)
                finish(i, far, jnp.exp2((s_buf[i] - m_all) * (SCALE * LOG2E)))

            both_kinds(weigh)

        inv = 1.0 / jnp.sum(ls[...], axis=1, keepdims=True)
        out = (o_acc[...] * inv).astype(jnp.bfloat16)
        for g in range(GROUP):
            o_out[j, :, g * HEAD : (g + 1) * HEAD] = out[g * BLOCK : (g + 1) * BLOCK]
        cot_low = (cotan.astype(jnp.float32) * inv).astype(jnp.bfloat16)
        delta = jnp.sum(cot_low.astype(jnp.float32) * out.astype(jnp.float32), axis=1, keepdims=True)
        mx[...] = jnp.broadcast_to(delta, (ROWS, HEAD))
        o_acc[...] = jnp.zeros((ROWS, HEAD), jnp.float32)
        d_rows[...] = cot_low
        d_cols[...] = jnp.concatenate([cot_low[g * BLOCK : (g + 1) * BLOCK].T for g in range(GROUP)], axis=1)

        def grads(i, far):
            key = keys(i, far)
            gw = nt(d_rows[...], values(i, far))
            d_all = jnp.concatenate([mx[...]] * CHUNK, axis=1)
            p_low = p_buf[i]
            ds = (gw - d_all).astype(jnp.bfloat16) * p_low
            o_acc[...] += nn(ds, key)
            dk = nn(q_cols[...], ds)
            dv = nn(d_cols[...], p_low)
            seg = tseg[i]
            for e in range(CHUNK):
                at = tblk[CHUNK * i] + e if far else tblk[CHUNK * i + e]
                acc[seg, at, :HEAD] += dk[:, e * BLOCK : (e + 1) * BLOCK]
                acc[seg, at, HEAD:] += dv[:, e * BLOCK : (e + 1) * BLOCK]

        both_kinds(grads)

        dq = (o_acc[...] * SCALE).astype(jnp.bfloat16)
        for g in range(GROUP):
            dq_out[j, :, g * HEAD : (g + 1) * HEAD] = dq[g * BLOCK : (g + 1) * BLOCK]

    flushes = []
    for w in (1, 0):
        route = core if w == 0 else 1 - core
        for outer, inner, ref, at in spans(parts[8 * w : 8 * w + 8]):
            src = stage.at[w, outer * 4 + inner]
            flushes.append(pltpu.make_async_copy(src, ref.at[at], out_sem.at[len(flushes)]))

        @pl.loop(0, nblk)
        def _(t):
            b = block_of(route, lax.div(t, 4), lax.rem(t, 4))
            for e in range(nseg):
                stage[w, t, e, :HEAD] = (acc[nseg * w + e, b, :HEAD] * SCALE).astype(jnp.bfloat16)
                stage[w, t, e, HEAD:] = acc[nseg * w + e, b, HEAD:].astype(jnp.bfloat16)

        for cp in flushes[-16:]:
            cp.start()
    for cp in flushes:
        cp.wait()


def attend(ids, parent, depth, both, pieces, side):
    nseg, nblk = both.shape[0], side * side
    groups = 3 * (nblk // CHUNK)
    vm = pl.BlockSpec(memory_space=pltpu.VMEM)
    hbm = pl.BlockSpec(memory_space=pl.ANY)
    sm = pl.BlockSpec(memory_space=pltpu.SMEM)
    bf = jnp.bfloat16
    f32 = jnp.float32
    parts = [jax.ShapeDtypeStruct((2, nseg, KVW, BLOCK), bf)] * 16
    return pl.pallas_call(
        functools.partial(attend_kernel, nseg, nblk, side),
        out_shape=[jax.ShapeDtypeStruct((nseg, BLOCK, ROWS), bf)] * 2 + parts,
        in_specs=[sm, sm, sm, vm] + [hbm] * 16,
        out_specs=[vm, vm] + [hbm] * 16,
        scratch_shapes=[
            pltpu.VMEM((2 * nseg, nblk, BLOCK, KVW), bf),
            pltpu.VMEM((2 * nseg, nblk + 1, KVW, BLOCK), f32),
            pltpu.VMEM((groups, ROWS, NKEY), f32),
            pltpu.VMEM((groups, ROWS, NKEY), bf),
            pltpu.VMEM((ROWS, HEAD), f32),
            pltpu.VMEM((ROWS, HEAD), f32),
            pltpu.VMEM((ROWS, HEAD), f32),
            pltpu.VMEM((ROWS, HEAD), bf),
            pltpu.VMEM((ROWS, HEAD), bf),
            pltpu.VMEM((HEAD, ROWS), bf),
            pltpu.VMEM((HEAD, ROWS), bf),
            pltpu.VMEM((2, nblk, nseg, KVW, BLOCK), bf),
            pltpu.SemaphoreType.DMA((32,)),
            pltpu.SemaphoreType.DMA((32,)),
            pltpu.SMEM((groups,), jnp.int32),
            pltpu.SMEM((groups * CHUNK,), jnp.int32),
        ],
        compiler_params=pltpu.CompilerParams(vmem_limit_bytes=62 * 1024 * 1024),
        cost_estimate=pl.CostEstimate(
            flops=nseg * 3 * nblk * BLOCK * ROWS * HEAD * 12,
            bytes_accessed=4 * nseg * nblk * BLOCK * KVW * 2,
            transcendentals=nseg * 3 * nblk * BLOCK * ROWS,
        ),
    )(ids, parent, depth, both, *pieces)


BOTH_AXES = ("cand", "ctx")


def ring(ncand, side, phase, step):
    pairs = []
    for c in range(ncand):
        along_x = (c % 2 == 1) == (phase == 0)
        for x in range(side):
            for z in range(side):
                to = ((x + step) % side, z) if along_x else (x, (z + step) % side)
                pairs.append(((c * side + x) * side + z, (c * side + to[0]) * side + to[1]))
    return pairs


def add(*xs):
    return functools.reduce(jnp.add, [x.astype(jnp.float32) for x in xs]).astype(jnp.bfloat16)


def hop(x, perm):
    return lax.ppermute(x, BOTH_AXES, perm)


def gather_ring(line_lo, line_hi, up, down):
    low_a = hop(line_lo, up)
    high_b = hop(line_hi, down)
    low_b = hop(line_hi, up)
    high_a = hop(line_lo, down)
    mid_a = hop(low_a, up)
    mid_b = hop(high_b, down)
    return [line_lo, line_hi, low_a, low_b, high_a, high_b, mid_a, mid_b]


def scatter_ring(own, came, up, down):
    same_lo, same_hi, low_a, low_b, high_a, high_b, mid_a, mid_b = zip(own, came)
    far_b, far_a = add(*mid_b), add(*mid_a)
    got_b = hop(far_b, up)
    got_a = hop(far_a, down)
    free_b, free_a = add(*low_b), add(*high_a)
    from_b = hop(free_b, down)
    from_a = hop(free_a, up)
    last_a, last_b = add(*low_a, got_a), add(*high_b, got_b)
    end_a = hop(last_a, down)
    end_b = hop(last_b, up)
    lo, hi = same_lo + (from_a, end_a), same_hi + (from_b, end_b)
    return [add(*[x[e] for x in part]) for part in (lo, hi) for e in range(2)]


def per_device(query_matrix, key_matrix, value_matrix, output_gradient, parent, seg_depth, block_mask):
    tok = query_matrix.shape[1]
    ncand = lax.axis_size("cand")
    nctx = lax.axis_size("ctx")
    nchip = ncand // 2
    heads = key_matrix.shape[2] // HEAD
    side = math.isqrt(nctx)
    pos = lax.axis_index("ctx")
    same_core = [[2 * y + c for y in range(nchip)] for c in range(2)]
    partner = [(i, i ^ 1) for i in range(ncand)]
    across = ring(ncand, side, 0, 2)
    rings = [(ring(ncand, side, phase, 1), ring(ncand, side, phase, -1)) for phase in range(2)]

    def spread(x):
        return lax.all_to_all(x, "cand", 0, 0, axis_index_groups=same_core)

    def cut(x, h, width):
        return x[:, h * width : (h + 1) * width]

    kv_own = jnp.stack(
        [
            jnp.concatenate([cut(key_matrix[0], h, HEAD), cut(value_matrix[0], h, HEAD)], axis=1)
            for h in range(heads)
        ]
    )
    kv_mine = spread(kv_own)
    near_low = hop(kv_mine, rings[0][0])
    near_high = hop(kv_mine, rings[0][1])
    opposite = hop(kv_mine, across)
    mine = gather_ring(jnp.stack([kv_mine, near_low]), jnp.stack([opposite, near_high]), *rings[1])
    pieces = mine + [lax.ppermute(x, "cand", partner) for x in mine]

    mask_row = lax.dynamic_index_in_dim(block_mask[0], pos, 0, keepdims=True).astype(jnp.bfloat16)
    extra = jnp.pad(mask_row, ((0, EXTRA - 1), (0, 2 * ROWS - nctx)))
    both = jnp.stack(
        [
            jnp.concatenate(
                [
                    jnp.concatenate(
                        [cut(query_matrix[0], h, ROWS), cut(output_gradient[0], h, ROWS)], axis=1
                    ),
                    extra,
                ],
                axis=0,
            )
            for h in range(heads)
        ]
    )
    both = spread(both)

    ids = jnp.stack([lax.axis_index("cand"), pos]).astype(jnp.int32)
    o, dq, *parts = attend(ids, parent, seg_depth, both, pieces, side)

    own, oth = parts[:8], parts[8:]
    came = [lax.ppermute(x, "cand", partner) for x in oth]
    to_self, to_low, to_far, to_high = scatter_ring(own, came, *rings[1])
    end_low = hop(to_low, rings[0][1])
    end_high = hop(to_high, rings[0][0])
    end_far = hop(to_far, across)
    summed = add(to_self, end_low, end_high, end_far)
    kv_grad = spread(summed)
    k_grad = kv_grad[:, :HEAD].transpose(2, 0, 1).reshape(1, tok, heads * HEAD)
    v_grad = kv_grad[:, HEAD:].transpose(2, 0, 1).reshape(1, tok, heads * HEAD)
    back = jnp.concatenate([o, dq], axis=2)
    back = spread(back)
    o_home = jnp.concatenate([back[h, :, :ROWS] for h in range(heads)], axis=1)[None]
    dq_home = jnp.concatenate([back[h, :, ROWS:] for h in range(heads)], axis=1)[None]
    return o_home, dq_home, k_grad, v_grad


def solution(mesh):
    split = P("cand", "ctx", None)
    return jax.shard_map(
        per_device,
        mesh=mesh,
        in_specs=(split, split, split, split, P(), P(), P("cand", None, None)),
        out_specs=(split, split, split, split),
        check_vma=False,
    )
```

```python
import functools
import math

import jax
import jax.numpy as jnp
from jax import lax
from jax.experimental import pallas as pl
from jax.experimental.pallas import tpu as pltpu
from jax.sharding import PartitionSpec as P


HEAD = 128
BLOCK = 128
GROUP = 3
ROWS = GROUP * BLOCK
KVW = 2 * HEAD
CHUNK = 4
NKEY = CHUNK * BLOCK
EXTRA = 16
NEG = -1e30
SCALE = HEAD ** (-0.5)
LOG2E = math.log2(math.e)
SAFE = 70.0


def nt(a, b):
    return lax.dot_general(a, b, (((1,), (1,)), ((), ())), preferred_element_type=jnp.float32)


def nn(a, b):
    return lax.dot_general(a, b, (((1,), (0,)), ((), ())), preferred_element_type=jnp.float32)


OUTER = (0, 0, 1, 1, 3, 3, 2, 2)


def spans(refs):
    return [(OUTER[k], 2 * (k % 2) + e, ref, e) for k, ref in enumerate(refs) for e in range(2)]


def attend_kernel(nseg, nblk, side, parent, depth, both, *refs):
    pieces, refs = refs[:16], refs[16:]
    o_out, dq_out = refs[:2]
    parts, refs = refs[2:18], refs[18:]
    kv, acc, s_buf, p_buf, mx, ls, o_acc, q_rows, d_rows, q_cols, d_cols, stage, in_sem, out_sem, tseg, tblk, tsrc = refs
    core = lax.rem(lax.axis_index("cand"), 2)
    pos = lax.axis_index("ctx")
    cx, cz = lax.div(pos, side), lax.rem(pos, side)

    def block_of(route, outer, inner):
        a = lax.rem(jnp.where(route == 0, cx, cz) + side - outer, side)
        b = lax.rem(jnp.where(route == 0, cz, cx) + side - inner, side)
        return jnp.where(route == 0, a * side + b, b * side + a)

    def place(s):
        return lax.div(s, 2) + jnp.where(lax.rem(s, 2) == core, 0, nseg)

    loads = []
    for w in range(2):
        route = core if w == 0 else 1 - core
        for outer, inner, ref, at in spans(pieces[8 * w : 8 * w + 8]):
            dst = kv.at[pl.ds(nseg * w, nseg), block_of(route, outer, inner)]
            loads.append(pltpu.make_async_copy(ref.at[at], dst, in_sem.at[len(loads)]))
    for cp in loads:
        cp.start()
    far_groups = nblk // CHUNK

    @pl.loop(0, 2 * nseg)
    def _(p):
        @pl.loop(0, nblk // 4)
        def _(b):
            for e in range(4):
                acc[p, 4 * b + e] = jnp.zeros((KVW, BLOCK), jnp.float32)

    def norm_step(p, top):
        tops = [jnp.abs(kv[p, b, :, :HEAD]) for b in range(nblk)]
        while len(tops) > 1:
            tops = [jnp.maximum(x, y) for x, y in zip(tops[::2], tops[1::2])]
        k = tops[0].astype(jnp.float32)
        k = jnp.max(k, axis=0, keepdims=True)
        return jnp.maximum(top, jnp.sum(k * k, axis=1, keepdims=True))

    key_top = jnp.zeros((1, 1), jnp.float32)
    for w in range(2):
        for cp in loads[nblk * w : nblk * (w + 1)]:
            cp.wait()
        key_top = lax.fori_loop(nseg * w, nseg * (w + 1), norm_step, key_top)

    def source(i, far, lo):
        if far:
            return kv[tseg[i], pl.ds(tblk[CHUNK * i], CHUNK), :, lo : lo + HEAD].reshape(NKEY, HEAD)
        at = [tsrc[CHUNK * i + e] for e in range(CHUNK)]
        return jnp.concatenate([kv[tseg[i], b, :, lo : lo + HEAD] for b in at], axis=0)

    def keys(i, far):
        return source(i, far, 0)

    def values(i, far):
        return source(i, far, HEAD)

    def lanes(op, x):
        return functools.reduce(op, [x[:, i * HEAD : (i + 1) * HEAD] for i in range(CHUNK)])

    @pl.loop(0, nseg)
    def _(j):
        qm = both[j, :BLOCK, :ROWS]
        dm = both[j, :BLOCK, ROWS:]
        rows_of = lambda x: jnp.concatenate([x[:, g * HEAD : (g + 1) * HEAD] for g in range(GROUP)], axis=0)
        query = rows_of(qm)
        cotan = rows_of(dm)
        q_rows[...] = query
        q_cols[...] = jnp.concatenate([qm[:, g * HEAD : (g + 1) * HEAD].T for g in range(GROUP)], axis=1)
        me = 2 * j + core
        nfar = depth[me]
        up = parent[me]
        far_a, far_b = place(up), place(parent[up])

        mask_row = both[j, BLOCK : BLOCK + EXTRA, :HEAD][:1].astype(jnp.float32)
        lane = lax.broadcasted_iota(jnp.int32, (1, HEAD), 1)
        bit = jnp.where((lane < nblk) & (mask_row > 0.5), jnp.left_shift(1, jnp.minimum(lane, nblk)), 0)
        code = jnp.sum(bit.astype(jnp.float32)).astype(jnp.int32)

        def add_own(b, n):
            tblk[n] = b
            tsrc[n] = b
            return n + lax.rem(jnp.right_shift(code, b), 2)

        seen = lax.fori_loop(0, pos, add_own, jnp.int32(0))
        own = lax.div(seen, CHUNK) + 1
        tail = seen - (own - 1) * CHUNK

        def add_tail(n, _):
            tblk[n] = jnp.where(n == seen, pos, nblk)
            tsrc[n] = pos
            return 0

        lax.fori_loop(seen, own * CHUNK, add_tail, 0)
        total = own + nfar * far_groups

        def add_seg(i, _):
            tseg[i] = jnp.where(i < own, j, jnp.where(i < own + far_groups, far_a, far_b))
            return 0

        lax.fori_loop(0, total, add_seg, 0)

        def add_far(n, _):
            tblk[(own + n) * CHUNK] = lax.rem(n, far_groups) * CHUNK
            return 0

        lax.fori_loop(0, nfar * far_groups, add_far, 0)

        ls[...] = jnp.zeros((ROWS, HEAD), jnp.float32)
        o_acc[...] = jnp.zeros((ROWS, HEAD), jnp.float32)

        qf = query.astype(jnp.float32)
        q_top = jnp.max(jnp.sum(qf * qf, axis=1, keepdims=True), axis=0, keepdims=True)
        small = jnp.max(q_top * key_top * (SCALE * SCALE)) <= SAFE * SAFE

        def scores(i, masked, far):
            s = nt(q_rows[...], keys(i, far))
            if masked:
                row = lax.broadcasted_iota(jnp.int32, (BLOCK, NKEY), 0)
                col = lax.broadcasted_iota(jnp.int32, (BLOCK, NKEY), 1)
                low = jnp.where(col <= row + tail * BLOCK, 0.0, NEG)
                s = s + jnp.concatenate([low] * GROUP, axis=0)
            return s

        def finish(i, far, p):
            ls[...] += lanes(jnp.add, p)
            p_low = p.astype(jnp.bfloat16)
            p_buf[i] = p_low
            o_acc[...] += nn(p_low, values(i, far))

        def both_kinds(body):
            @pl.loop(0, own)
            def _(i):
                body(i, False)

            @pl.loop(own, total)
            def _(i):
                body(i, True)

        def sweep(body):
            body(own - 1, True, False)

            @pl.loop(0, own - 1)
            def _(i):
                body(i, False, False)

            @pl.loop(own, total)
            def _(i):
                body(i, False, True)

        @pl.when(small)
        def _():
            sweep(lambda i, masked, far: finish(i, far, jnp.exp2(scores(i, masked, far) * (SCALE * LOG2E))))

        @pl.when(jnp.logical_not(small))
        def _():
            mx[...] = jnp.full((ROWS, HEAD), NEG, jnp.float32)

            def body(i, masked, far):
                s = scores(i, masked, far)
                s_buf[i] = s
                mx[...] = jnp.maximum(mx[...], lanes(jnp.maximum, s))

            sweep(body)
            top = jnp.max(mx[...], axis=1, keepdims=True)
            mx[...] = jnp.broadcast_to(top, (ROWS, HEAD))

            def weigh(i, far):
                m_all = jnp.concatenate([mx[...]] * CHUNK, axis=1)
                finish(i, far, jnp.exp2((s_buf[i] - m_all) * (SCALE * LOG2E)))

            both_kinds(weigh)

        inv = 1.0 / jnp.sum(ls[...], axis=1, keepdims=True)
        out = (o_acc[...] * inv).astype(jnp.bfloat16)
        for g in range(GROUP):
            o_out[j, :, g * HEAD : (g + 1) * HEAD] = out[g * BLOCK : (g + 1) * BLOCK]
        cot_low = (cotan.astype(jnp.float32) * inv).astype(jnp.bfloat16)
        delta = jnp.sum(cot_low.astype(jnp.float32) * out.astype(jnp.float32), axis=1, keepdims=True)
        mx[...] = jnp.broadcast_to(delta, (ROWS, HEAD))
        o_acc[...] = jnp.zeros((ROWS, HEAD), jnp.float32)
        d_rows[...] = cot_low
        d_cols[...] = jnp.concatenate([cot_low[g * BLOCK : (g + 1) * BLOCK].T for g in range(GROUP)], axis=1)

        def grads(i, far):
            key = keys(i, far)
            gw = nt(d_rows[...], values(i, far))
            d_all = jnp.concatenate([mx[...]] * CHUNK, axis=1)
            p_low = p_buf[i]
            ds = (gw - d_all).astype(jnp.bfloat16) * p_low
            o_acc[...] += nn(ds, key)
            dk = nn(q_cols[...], ds)
            dv = nn(d_cols[...], p_low)
            seg = tseg[i]
            for e in range(CHUNK):
                at = tblk[CHUNK * i] + e if far else tblk[CHUNK * i + e]
                acc[seg, at, :HEAD] += dk[:, e * BLOCK : (e + 1) * BLOCK]
                acc[seg, at, HEAD:] += dv[:, e * BLOCK : (e + 1) * BLOCK]

        both_kinds(grads)

        dq = (o_acc[...] * SCALE).astype(jnp.bfloat16)
        for g in range(GROUP):
            dq_out[j, :, g * HEAD : (g + 1) * HEAD] = dq[g * BLOCK : (g + 1) * BLOCK]

    flushes = []
    for w in (1, 0):
        route = core if w == 0 else 1 - core
        found = spans(parts[8 * w : 8 * w + 8])
        for outer in (2, 1, 3, 0):
            for inner in range(4):
                b = block_of(route, outer, inner)
                t = outer * 4 + inner
                for e in range(nseg):
                    stage[w, t, e, :HEAD] = (acc[nseg * w + e, b, :HEAD] * SCALE).astype(jnp.bfloat16)
                    stage[w, t, e, HEAD:] = acc[nseg * w + e, b, HEAD:].astype(jnp.bfloat16)
            for o, inner, ref, at in found:
                if o == outer:
                    src = stage.at[w, outer * 4 + inner]
                    cp = pltpu.make_async_copy(src, ref.at[at], out_sem.at[len(flushes)])
                    cp.start()
                    flushes.append(cp)
    for cp in flushes:
        cp.wait()


def attend(parent, depth, both, pieces, side):
    nseg, nblk = both.shape[0], side * side
    groups = 3 * (nblk // CHUNK)
    vm = pl.BlockSpec(memory_space=pltpu.VMEM)
    hbm = pl.BlockSpec(memory_space=pl.ANY)
    sm = pl.BlockSpec(memory_space=pltpu.SMEM)
    bf = jnp.bfloat16
    f32 = jnp.float32
    parts = [jax.ShapeDtypeStruct((2, nseg, KVW, BLOCK), bf)] * 16
    return pl.pallas_call(
        functools.partial(attend_kernel, nseg, nblk, side),
        out_shape=[jax.ShapeDtypeStruct((nseg, BLOCK, ROWS), bf)] * 2 + parts,
        in_specs=[sm, sm, vm] + [hbm] * 16,
        out_specs=[vm, vm] + [hbm] * 16,
        scratch_shapes=[
            pltpu.VMEM((2 * nseg, nblk, BLOCK, KVW), bf),
            pltpu.VMEM((2 * nseg, nblk + 1, KVW, BLOCK), f32),
            pltpu.VMEM((groups, ROWS, NKEY), f32),
            pltpu.VMEM((groups, ROWS, NKEY), bf),
            pltpu.VMEM((ROWS, HEAD), f32),
            pltpu.VMEM((ROWS, HEAD), f32),
            pltpu.VMEM((ROWS, HEAD), f32),
            pltpu.VMEM((ROWS, HEAD), bf),
            pltpu.VMEM((ROWS, HEAD), bf),
            pltpu.VMEM((HEAD, ROWS), bf),
            pltpu.VMEM((HEAD, ROWS), bf),
            pltpu.VMEM((2, nblk, nseg, KVW, BLOCK), bf),
            pltpu.SemaphoreType.DMA((32,)),
            pltpu.SemaphoreType.DMA((32,)),
            pltpu.SMEM((groups,), jnp.int32),
            pltpu.SMEM((groups * CHUNK,), jnp.int32),
            pltpu.SMEM((groups * CHUNK,), jnp.int32),
        ],
        compiler_params=pltpu.CompilerParams(vmem_limit_bytes=62 * 1024 * 1024),
        cost_estimate=pl.CostEstimate(
            flops=nseg * 3 * nblk * BLOCK * ROWS * HEAD * 12,
            bytes_accessed=4 * nseg * nblk * BLOCK * KVW * 2,
            transcendentals=nseg * 3 * nblk * BLOCK * ROWS,
        ),
    )(parent, depth, both, *pieces)


BOTH_AXES = ("cand", "ctx")


def ring(ncand, side, phase, step):
    pairs = []
    for c in range(ncand):
        along_x = (c % 2 == 1) == (phase == 0)
        for x in range(side):
            for z in range(side):
                to = ((x + step) % side, z) if along_x else (x, (z + step) % side)
                pairs.append(((c * side + x) * side + z, (c * side + to[0]) * side + to[1]))
    return pairs


def add(*xs):
    return functools.reduce(jnp.add, [x.astype(jnp.float32) for x in xs]).astype(jnp.bfloat16)


def hop(x, perm):
    return lax.ppermute(x, BOTH_AXES, perm)


def gather_ring(line_lo, line_hi, up, down):
    low_a = hop(line_lo, up)
    high_b = hop(line_hi, down)
    low_b = hop(line_hi, up)
    high_a = hop(line_lo, down)
    mid_a = hop(low_a, up)
    mid_b = hop(high_b, down)
    return [line_lo, line_hi, low_a, low_b, high_a, high_b, mid_a, mid_b]


def scatter_ring(own, came, up, down):
    same_lo, same_hi, low_a, low_b, high_a, high_b, mid_a, mid_b = zip(own, came)
    far_b, far_a = add(*mid_b), add(*mid_a)
    got_b = hop(far_b, up)
    got_a = hop(far_a, down)
    free_b, free_a = add(*low_b), add(*high_a)
    from_b = hop(free_b, down)
    from_a = hop(free_a, up)
    last_a, last_b = add(*low_a, got_a), add(*high_b, got_b)
    end_a = hop(last_a, down)
    end_b = hop(last_b, up)
    lo, hi = same_lo + (from_a, end_a), same_hi + (from_b, end_b)
    return [add(*[x[e] for x in part]) for part in (lo, hi) for e in range(2)]


def per_device(query_matrix, key_matrix, value_matrix, output_gradient, parent, seg_depth, block_mask):
    tok = query_matrix.shape[1]
    ncand = lax.axis_size("cand")
    nctx = lax.axis_size("ctx")
    nchip = ncand // 2
    heads = key_matrix.shape[2] // HEAD
    side = math.isqrt(nctx)
    pos = lax.axis_index("ctx")
    same_core = [[2 * y + c for y in range(nchip)] for c in range(2)]
    partner = [(i, i ^ 1) for i in range(ncand)]
    across = ring(ncand, side, 0, 2)
    rings = [(ring(ncand, side, phase, 1), ring(ncand, side, phase, -1)) for phase in range(2)]

    def spread(x):
        return lax.all_to_all(x, "cand", 0, 0, axis_index_groups=same_core)

    def cut(x, h, width):
        return x[:, h * width : (h + 1) * width]

    kv_own = jnp.stack(
        [
            jnp.concatenate([cut(key_matrix[0], h, HEAD), cut(value_matrix[0], h, HEAD)], axis=1)
            for h in range(heads)
        ]
    )
    kv_mine = spread(kv_own)
    near_low = hop(kv_mine, rings[0][0])
    near_high = hop(kv_mine, rings[0][1])
    opposite = hop(kv_mine, across)
    mine = gather_ring(jnp.stack([kv_mine, near_low]), jnp.stack([opposite, near_high]), *rings[1])
    pieces = mine + [lax.ppermute(x, "cand", partner) for x in mine]

    mask_row = lax.dynamic_index_in_dim(block_mask[0], pos, 0, keepdims=True).astype(jnp.bfloat16)
    extra = jnp.pad(mask_row, ((0, EXTRA - 1), (0, 2 * ROWS - nctx)))
    both = jnp.stack(
        [
            jnp.concatenate(
                [
                    jnp.concatenate(
                        [cut(query_matrix[0], h, ROWS), cut(output_gradient[0], h, ROWS)], axis=1
                    ),
                    extra,
                ],
                axis=0,
            )
            for h in range(heads)
        ]
    )
    both = spread(both)

    o, dq, *parts = attend(parent, seg_depth, both, pieces, side)

    own, oth = parts[:8], parts[8:]
    came = [lax.ppermute(x, "cand", partner) for x in oth]
    to_self, to_low, to_far, to_high = scatter_ring(own, came, *rings[1])
    end_low = hop(to_low, rings[0][1])
    end_high = hop(to_high, rings[0][0])
    end_far = hop(to_far, across)
    summed = add(to_self, end_low, end_high, end_far)
    kv_grad = spread(summed)
    k_grad = kv_grad[:, :HEAD].transpose(2, 0, 1).reshape(1, tok, heads * HEAD)
    v_grad = kv_grad[:, HEAD:].transpose(2, 0, 1).reshape(1, tok, heads * HEAD)
    back = jnp.concatenate([o, dq], axis=2)
    back = spread(back)
    o_home = jnp.concatenate([back[h, :, :ROWS] for h in range(heads)], axis=1)[None]
    dq_home = jnp.concatenate([back[h, :, ROWS:] for h in range(heads)], axis=1)[None]
    return o_home, dq_home, k_grad, v_grad


def solution(mesh):
    split = P("cand", "ctx", None)
    return jax.shard_map(
        per_device,
        mesh=mesh,
        in_specs=(split, split, split, split, P(), P(), P("cand", None, None)),
        out_specs=(split, split, split, split),
        check_vma=False,
    )
```

```python
import functools
import math

import jax
import jax.numpy as jnp
from jax import lax
from jax.experimental import pallas as pl
from jax.experimental.pallas import tpu as pltpu
from jax.sharding import PartitionSpec as P


HEAD = 128
BLOCK = 128
GROUP = 3
ROWS = GROUP * BLOCK
KVW = 2 * HEAD
CHUNK = 4
NKEY = CHUNK * BLOCK
EXTRA = 16
NEG = -1e30
SCALE = HEAD ** (-0.5)
LOG2E = math.log2(math.e)
SAFE = 70.0


def nt(a, b):
    return lax.dot_general(a, b, (((1,), (1,)), ((), ())), preferred_element_type=jnp.float32)


def nn(a, b):
    return lax.dot_general(a, b, (((1,), (0,)), ((), ())), preferred_element_type=jnp.float32)


OUTER = (0, 0, 1, 1, 3, 3, 2, 2)


def spans(refs):
    return [(OUTER[k], 2 * (k % 2) + e, ref, e) for k, ref in enumerate(refs) for e in range(2)]


def attend_kernel(nseg, nblk, side, parent, depth, both, *refs):
    pieces, refs = refs[:16], refs[16:]
    o_out, dq_out = refs[:2]
    parts, refs = refs[2:18], refs[18:]
    kv, acc, s_buf, p_buf, mx, ls, o_acc, q_rows, d_rows, q_cols, d_cols, stage, in_sem, out_sem, tseg, tblk, tsrc = refs
    core = lax.rem(lax.axis_index("cand"), 2)
    pos = lax.axis_index("ctx")
    cx, cz = lax.div(pos, side), lax.rem(pos, side)

    def block_of(route, outer, inner):
        a = lax.rem(jnp.where(route == 0, cx, cz) + side - outer, side)
        b = lax.rem(jnp.where(route == 0, cz, cx) + side - inner, side)
        return jnp.where(route == 0, a * side + b, b * side + a)

    def place(s):
        return lax.div(s, 2) + jnp.where(lax.rem(s, 2) == core, 0, nseg)

    loads = []
    for w in range(2):
        route = core if w == 0 else 1 - core
        for outer, inner, ref, at in spans(pieces[8 * w : 8 * w + 8]):
            dst = kv.at[pl.ds(nseg * w, nseg), block_of(route, outer, inner)]
            loads.append(pltpu.make_async_copy(ref.at[at], dst, in_sem.at[len(loads)]))
    for cp in loads:
        cp.start()
    far_groups = nblk // CHUNK

    @pl.loop(0, 2 * nseg)
    def _(p):
        @pl.loop(0, nblk // 4)
        def _(b):
            for e in range(4):
                acc[p, 4 * b + e] = jnp.zeros((KVW, BLOCK), jnp.float32)

    def norm_step(p, top):
        tops = [jnp.abs(kv[p, b, :, :HEAD]) for b in range(nblk)]
        while len(tops) > 1:
            tops = [jnp.maximum(x, y) for x, y in zip(tops[::2], tops[1::2])]
        k = tops[0].astype(jnp.float32)
        k = jnp.max(k, axis=0, keepdims=True)
        return jnp.maximum(top, jnp.sum(k * k, axis=1, keepdims=True))

    key_top = jnp.zeros((1, 1), jnp.float32)
    for w in range(2):
        for cp in loads[nblk * w : nblk * (w + 1)]:
            cp.wait()
        key_top = lax.fori_loop(nseg * w, nseg * (w + 1), norm_step, key_top)

    def source(i, far, lo):
        if far:
            return kv[tseg[i], pl.ds(tblk[CHUNK * i], CHUNK), :, lo : lo + HEAD].reshape(NKEY, HEAD)
        at = [tsrc[CHUNK * i + e] for e in range(CHUNK)]
        return jnp.concatenate([kv[tseg[i], b, :, lo : lo + HEAD] for b in at], axis=0)

    def keys(i, far):
        return source(i, far, 0)

    def values(i, far):
        return source(i, far, HEAD)

    def lanes(op, x):
        return functools.reduce(op, [x[:, i * HEAD : (i + 1) * HEAD] for i in range(CHUNK)])

    @pl.loop(0, nseg)
    def _(j):
        qm = both[j, :BLOCK, :ROWS]
        dm = both[j, :BLOCK, ROWS:]
        rows_of = lambda x: jnp.concatenate([x[:, g * HEAD : (g + 1) * HEAD] for g in range(GROUP)], axis=0)
        query = rows_of(qm)
        cotan = rows_of(dm)
        q_rows[...] = query
        q_cols[...] = jnp.concatenate([qm[:, g * HEAD : (g + 1) * HEAD].T for g in range(GROUP)], axis=1)
        me = 2 * j + core
        nfar = depth[me]
        up = parent[me]
        far_a, far_b = place(up), place(parent[up])

        mask_row = both[j, BLOCK : BLOCK + EXTRA, :HEAD][:1].astype(jnp.float32)
        lane = lax.broadcasted_iota(jnp.int32, (1, HEAD), 1)
        bit = jnp.where((lane < nblk) & (mask_row > 0.5), jnp.left_shift(1, jnp.minimum(lane, nblk)), 0)
        code = jnp.sum(bit.astype(jnp.float32)).astype(jnp.int32)

        def add_own(b, n):
            tblk[n] = b
            tsrc[n] = b
            return n + lax.rem(jnp.right_shift(code, b), 2)

        seen = lax.fori_loop(0, pos, add_own, jnp.int32(0))
        own = lax.div(seen, CHUNK) + 1
        tail = seen - (own - 1) * CHUNK

        def add_tail(n, _):
            tblk[n] = jnp.where(n == seen, pos, nblk)
            tsrc[n] = pos
            return 0

        lax.fori_loop(seen, own * CHUNK, add_tail, 0)
        total = own + nfar * far_groups

        def add_seg(i, _):
            tseg[i] = jnp.where(i < own, j, jnp.where(i < own + far_groups, far_a, far_b))
            return 0

        lax.fori_loop(0, total, add_seg, 0)

        def add_far(n, _):
            tblk[(own + n) * CHUNK] = lax.rem(n, far_groups) * CHUNK
            return 0

        lax.fori_loop(0, nfar * far_groups, add_far, 0)

        ls[...] = jnp.zeros((ROWS, HEAD), jnp.float32)
        o_acc[...] = jnp.zeros((ROWS, HEAD), jnp.float32)

        qf = query.astype(jnp.float32)
        q_top = jnp.max(jnp.sum(qf * qf, axis=1, keepdims=True), axis=0, keepdims=True)
        small = jnp.max(q_top * key_top * (SCALE * SCALE)) <= SAFE * SAFE

        def scores(i, masked, far):
            s = nt(q_rows[...], keys(i, far))
            if masked:
                row = lax.broadcasted_iota(jnp.int32, (BLOCK, NKEY), 0)
                col = lax.broadcasted_iota(jnp.int32, (BLOCK, NKEY), 1)
                low = jnp.where(col <= row + tail * BLOCK, 0.0, NEG)
                s = s + jnp.concatenate([low] * GROUP, axis=0)
            return s

        def finish(i, far, p):
            ls[...] += lanes(jnp.add, p)
            p_low = p.astype(jnp.bfloat16)
            p_buf[i] = p_low
            o_acc[...] += nn(p_low, values(i, far))

        def both_kinds(body):
            @pl.loop(0, own)
            def _(i):
                body(i, False)

            @pl.loop(0, lax.div(total - own, 2))
            def _(n):
                body(own + 2 * n, True)
                body(own + 2 * n + 1, True)

        def sweep(body):
            body(own - 1, True, False)

            @pl.loop(0, own - 1)
            def _(i):
                body(i, False, False)

            @pl.loop(0, lax.div(total - own, 2))
            def _(n):
                body(own + 2 * n, False, True)
                body(own + 2 * n + 1, False, True)

        @pl.when(small)
        def _():
            sweep(lambda i, masked, far: finish(i, far, jnp.exp2(scores(i, masked, far) * (SCALE * LOG2E))))

        @pl.when(jnp.logical_not(small))
        def _():
            mx[...] = jnp.full((ROWS, HEAD), NEG, jnp.float32)

            def body(i, masked, far):
                s = scores(i, masked, far)
                s_buf[i] = s
                mx[...] = jnp.maximum(mx[...], lanes(jnp.maximum, s))

            sweep(body)
            top = jnp.max(mx[...], axis=1, keepdims=True)
            mx[...] = jnp.broadcast_to(top, (ROWS, HEAD))

            def weigh(i, far):
                m_all = jnp.concatenate([mx[...]] * CHUNK, axis=1)
                finish(i, far, jnp.exp2((s_buf[i] - m_all) * (SCALE * LOG2E)))

            both_kinds(weigh)

        inv = 1.0 / jnp.sum(ls[...], axis=1, keepdims=True)
        out = (o_acc[...] * inv).astype(jnp.bfloat16)
        for g in range(GROUP):
            o_out[j, :, g * HEAD : (g + 1) * HEAD] = out[g * BLOCK : (g + 1) * BLOCK]
        cot_low = (cotan.astype(jnp.float32) * inv).astype(jnp.bfloat16)
        delta = jnp.sum(cot_low.astype(jnp.float32) * out.astype(jnp.float32), axis=1, keepdims=True)
        mx[...] = jnp.broadcast_to(delta, (ROWS, HEAD))
        o_acc[...] = jnp.zeros((ROWS, HEAD), jnp.float32)
        d_rows[...] = cot_low
        d_cols[...] = jnp.concatenate([cot_low[g * BLOCK : (g + 1) * BLOCK].T for g in range(GROUP)], axis=1)

        def grads(i, far):
            key = keys(i, far)
            gw = nt(d_rows[...], values(i, far))
            d_all = jnp.concatenate([mx[...]] * CHUNK, axis=1)
            p_low = p_buf[i]
            ds = (gw - d_all).astype(jnp.bfloat16) * p_low
            o_acc[...] += nn(ds, key)
            dk = nn(q_cols[...], ds)
            dv = nn(d_cols[...], p_low)
            seg = tseg[i]
            for e in range(CHUNK):
                at = tblk[CHUNK * i] + e if far else tblk[CHUNK * i + e]
                acc[seg, at, :HEAD] += dk[:, e * BLOCK : (e + 1) * BLOCK]
                acc[seg, at, HEAD:] += dv[:, e * BLOCK : (e + 1) * BLOCK]

        both_kinds(grads)

        dq = (o_acc[...] * SCALE).astype(jnp.bfloat16)
        for g in range(GROUP):
            dq_out[j, :, g * HEAD : (g + 1) * HEAD] = dq[g * BLOCK : (g + 1) * BLOCK]

    flushes = []
    for w in (1, 0):
        route = core if w == 0 else 1 - core
        found = spans(parts[8 * w : 8 * w + 8])
        for outer in (2, 1, 3, 0):
            for inner in range(4):
                b = block_of(route, outer, inner)
                t = outer * 4 + inner
                for e in range(nseg):
                    stage[w, t, e, :HEAD] = (acc[nseg * w + e, b, :HEAD] * SCALE).astype(jnp.bfloat16)
                    stage[w, t, e, HEAD:] = acc[nseg * w + e, b, HEAD:].astype(jnp.bfloat16)
            for o, inner, ref, at in found:
                if o == outer:
                    src = stage.at[w, outer * 4 + inner]
                    cp = pltpu.make_async_copy(src, ref.at[at], out_sem.at[len(flushes)])
                    cp.start()
                    flushes.append(cp)
    for cp in flushes:
        cp.wait()


def attend(parent, depth, both, pieces, side):
    nseg, nblk = both.shape[0], side * side
    groups = 3 * (nblk // CHUNK)
    vm = pl.BlockSpec(memory_space=pltpu.VMEM)
    hbm = pl.BlockSpec(memory_space=pl.ANY)
    sm = pl.BlockSpec(memory_space=pltpu.SMEM)
    bf = jnp.bfloat16
    f32 = jnp.float32
    parts = [jax.ShapeDtypeStruct((2, nseg, KVW, BLOCK), bf)] * 16
    return pl.pallas_call(
        functools.partial(attend_kernel, nseg, nblk, side),
        out_shape=[jax.ShapeDtypeStruct((nseg, BLOCK, ROWS), bf)] * 2 + parts,
        in_specs=[sm, sm, vm] + [hbm] * 16,
        out_specs=[vm, vm] + [hbm] * 16,
        scratch_shapes=[
            pltpu.VMEM((2 * nseg, nblk, BLOCK, KVW), bf),
            pltpu.VMEM((2 * nseg, nblk + 1, KVW, BLOCK), f32),
            pltpu.VMEM((groups, ROWS, NKEY), f32),
            pltpu.VMEM((groups, ROWS, NKEY), bf),
            pltpu.VMEM((ROWS, HEAD), f32),
            pltpu.VMEM((ROWS, HEAD), f32),
            pltpu.VMEM((ROWS, HEAD), f32),
            pltpu.VMEM((ROWS, HEAD), bf),
            pltpu.VMEM((ROWS, HEAD), bf),
            pltpu.VMEM((HEAD, ROWS), bf),
            pltpu.VMEM((HEAD, ROWS), bf),
            pltpu.VMEM((2, nblk, nseg, KVW, BLOCK), bf),
            pltpu.SemaphoreType.DMA((32,)),
            pltpu.SemaphoreType.DMA((32,)),
            pltpu.SMEM((groups,), jnp.int32),
            pltpu.SMEM((groups * CHUNK,), jnp.int32),
            pltpu.SMEM((groups * CHUNK,), jnp.int32),
        ],
        compiler_params=pltpu.CompilerParams(vmem_limit_bytes=62 * 1024 * 1024),
        cost_estimate=pl.CostEstimate(
            flops=nseg * 3 * nblk * BLOCK * ROWS * HEAD * 12,
            bytes_accessed=4 * nseg * nblk * BLOCK * KVW * 2,
            transcendentals=nseg * 3 * nblk * BLOCK * ROWS,
        ),
    )(parent, depth, both, *pieces)


BOTH_AXES = ("cand", "ctx")


def ring(ncand, side, phase, step):
    pairs = []
    for c in range(ncand):
        along_x = (c % 2 == 1) == (phase == 0)
        for x in range(side):
            for z in range(side):
                to = ((x + step) % side, z) if along_x else (x, (z + step) % side)
                pairs.append(((c * side + x) * side + z, (c * side + to[0]) * side + to[1]))
    return pairs


def add(*xs):
    return functools.reduce(jnp.add, [x.astype(jnp.float32) for x in xs]).astype(jnp.bfloat16)


def hop(x, perm):
    return lax.ppermute(x, BOTH_AXES, perm)


def gather_ring(line_lo, line_hi, up, down):
    low_a = hop(line_lo, up)
    high_b = hop(line_hi, down)
    low_b = hop(line_hi, up)
    high_a = hop(line_lo, down)
    mid_a = hop(low_a, up)
    mid_b = hop(high_b, down)
    return [line_lo, line_hi, low_a, low_b, high_a, high_b, mid_a, mid_b]


def scatter_ring(own, came, up, down):
    same_lo, same_hi, low_a, low_b, high_a, high_b, mid_a, mid_b = zip(own, came)
    far_b, far_a = add(*mid_b), add(*mid_a)
    got_b = hop(far_b, up)
    got_a = hop(far_a, down)
    free_b, free_a = add(*low_b), add(*high_a)
    from_b = hop(free_b, down)
    from_a = hop(free_a, up)
    last_a, last_b = add(*low_a, got_a), add(*high_b, got_b)
    end_a = hop(last_a, down)
    end_b = hop(last_b, up)
    lo, hi = same_lo + (from_a, end_a), same_hi + (from_b, end_b)
    return [add(*[x[e] for x in part]) for part in (lo, hi) for e in range(2)]


def per_device(query_matrix, key_matrix, value_matrix, output_gradient, parent, seg_depth, block_mask):
    tok = query_matrix.shape[1]
    ncand = lax.axis_size("cand")
    nctx = lax.axis_size("ctx")
    nchip = ncand // 2
    heads = key_matrix.shape[2] // HEAD
    side = math.isqrt(nctx)
    pos = lax.axis_index("ctx")
    same_core = [[2 * y + c for y in range(nchip)] for c in range(2)]
    partner = [(i, i ^ 1) for i in range(ncand)]
    across = ring(ncand, side, 0, 2)
    rings = [(ring(ncand, side, phase, 1), ring(ncand, side, phase, -1)) for phase in range(2)]

    def spread(x):
        return lax.all_to_all(x, "cand", 0, 0, axis_index_groups=same_core)

    def cut(x, h, width):
        return x[:, h * width : (h + 1) * width]

    kv_own = jnp.stack(
        [
            jnp.concatenate([cut(key_matrix[0], h, HEAD), cut(value_matrix[0], h, HEAD)], axis=1)
            for h in range(heads)
        ]
    )
    kv_mine = spread(kv_own)
    near_low = hop(kv_mine, rings[0][0])
    near_high = hop(kv_mine, rings[0][1])
    opposite = hop(kv_mine, across)
    mine = gather_ring(jnp.stack([kv_mine, near_low]), jnp.stack([opposite, near_high]), *rings[1])
    pieces = mine + [lax.ppermute(x, "cand", partner) for x in mine]

    mask_row = lax.dynamic_index_in_dim(block_mask[0], pos, 0, keepdims=True).astype(jnp.bfloat16)
    extra = jnp.pad(mask_row, ((0, EXTRA - 1), (0, 2 * ROWS - nctx)))
    both = jnp.stack(
        [
            jnp.concatenate(
                [
                    jnp.concatenate(
                        [cut(query_matrix[0], h, ROWS), cut(output_gradient[0], h, ROWS)], axis=1
                    ),
                    extra,
                ],
                axis=0,
            )
            for h in range(heads)
        ]
    )
    both = spread(both)

    o, dq, *parts = attend(parent, seg_depth, both, pieces, side)

    own, oth = parts[:8], parts[8:]
    came = [lax.ppermute(x, "cand", partner) for x in oth]
    to_self, to_low, to_far, to_high = scatter_ring(own, came, *rings[1])
    end_low = hop(to_low, rings[0][1])
    end_high = hop(to_high, rings[0][0])
    end_far = hop(to_far, across)
    summed = add(to_self, end_low, end_high, end_far)
    kv_grad = spread(summed)
    k_grad = kv_grad[:, :HEAD].transpose(2, 0, 1).reshape(1, tok, heads * HEAD)
    v_grad = kv_grad[:, HEAD:].transpose(2, 0, 1).reshape(1, tok, heads * HEAD)
    back = jnp.concatenate([o, dq], axis=2)
    back = spread(back)
    o_home = jnp.concatenate([back[h, :, :ROWS] for h in range(heads)], axis=1)[None]
    dq_home = jnp.concatenate([back[h, :, ROWS:] for h in range(heads)], axis=1)[None]
    return o_home, dq_home, k_grad, v_grad


def solution(mesh):
    split = P("cand", "ctx", None)
    return jax.shard_map(
        per_device,
        mesh=mesh,
        in_specs=(split, split, split, split, P(), P(), P("cand", None, None)),
        out_specs=(split, split, split, split),
        check_vma=False,
    )
```
